256 devices in a mesh: blk: 128 (over z, y, x_lo, core), tok: 2 (over x_hi).
Axes of the slice: x: 4 (x_hi: 2, x_lo: 2; x = x_hi * 2 + x_lo), y: 4, z: 8, core: 2. Of those that a mesh axis runs over, the one named last changes fastest.
Arguments:
- tokens: bfloat16 [512, 8192], P(('blk', 'tok')), may hold values from -6 to 6
- upstream: bfloat16 [512, 8192], P(('blk', 'tok')), may hold values from -6 to 6
- gate_weight: bfloat16 [14336, 8192], P('blk'), may hold values from -0.0625 to 0.0625
- up_weight: bfloat16 [14336, 8192], P('blk'), may hold values from -0.0625 to 0.0625
- down_weight: bfloat16 [14336, 8192], P('blk'), may hold values from -0.046875 to 0.046875
Outputs:
- mixed: bfloat16 [512, 8192], P(('blk', 'tok'))
- input_grad: bfloat16 [512, 8192], P(('blk', 'tok'))
- gate_weight_grad: bfloat16 [14336, 8192], P('blk', 'tok')
- up_weight_grad: bfloat16 [14336, 8192], P('blk', 'tok')
- down_weight_grad: bfloat16 [14336, 8192], P('blk', 'tok')
The draws below stay inside these ranges and needn't reach their ends.
All inputs are finite; a program needn't handle non-finite values.
Results may differ from the reference program's by a relative error of at most 0.0049.
Values may be sent and summed in bfloat16 or wider, within the bound.
No kernel may reach another device: no remote copies, remote signals or barrier semaphores. Data moves between devices by JAX's collectives and lax.ppermute only.
A program may use at most 128 MiB of HBM per device.

```python
import jax
import jax.numpy as jnp

D = 8192
FF = 14336
TOKENS = 512


def level_of(own_key, extent, shards, low, high):
    gain = 1.0
    for dim, shards_of in shards:
        draws = jax.random.uniform(jax.random.fold_in(jax.random.fold_in(own_key, 6), dim), (shards_of,), jnp.float32, low / len(shards), high / len(shards))
        gain = gain * jnp.repeat(jnp.exp(draws), extent[dim] // shards_of).reshape((-1,) + (1,) * (len(extent) - 1 - dim))
    return gain


def noise(own_key, shape, scale, most, pieces=(), kind=jnp.bfloat16):
    level = level_of(own_key, shape, pieces, -0.22, 0.18) if pieces else 1.0
    drawn = jax.random.normal(own_key, shape, jnp.float32) * scale * level
    return jnp.minimum(jnp.maximum(drawn, -most), most).astype(kind)


def setup_inputs(seed: int = 0) -> dict:
    streams_of = jax.random.split(jax.random.key(seed), 6)
    tokens = noise(streams_of[0], (TOKENS, D), 1.0, 6.0, ((0, 256),))
    upstream = noise(streams_of[1], (TOKENS, D), 1.0, 6.0, ((0, 256),))
    gate_weight = noise(streams_of[2], (FF, D), D ** -0.5, 0.0625, ((0, 128),))
    up_weight = noise(streams_of[3], (FF, D), D ** -0.5, 0.0625, ((0, 128),))
    down_weight = noise(streams_of[4], (FF, D), FF ** -0.5, 0.046875, ((0, 128),))
    return dict(tokens=tokens, upstream=upstream, gate_weight=gate_weight, up_weight=up_weight, down_weight=down_weight)


def reference(tokens, upstream, gate_weight, up_weight, down_weight):
    gate_value = jnp.dot(tokens, gate_weight.T, preferred_element_type=jnp.float32)
    up_value = jnp.dot(tokens, up_weight.T, preferred_element_type=jnp.float32)
    gate_sigmoid = jax.nn.sigmoid(gate_value)
    swish_gate = gate_value * gate_sigmoid
    hidden = (swish_gate * up_value).astype(jnp.bfloat16)
    mixed = jnp.dot(hidden, down_weight, preferred_element_type=jnp.float32).astype(jnp.bfloat16)
    hidden_grad = jnp.dot(upstream, down_weight.T, preferred_element_type=jnp.float32)
    gate_grad = (hidden_grad * up_value * gate_sigmoid * (1.0 + gate_value * (1.0 - gate_sigmoid))).astype(jnp.bfloat16)
    up_grad = (hidden_grad * swish_gate).astype(jnp.bfloat16)
    input_sum = jnp.dot(gate_grad, gate_weight, preferred_element_type=jnp.float32)
    input_sum = input_sum + jnp.dot(up_grad, up_weight, preferred_element_type=jnp.float32)
    input_grad = input_sum.astype(jnp.bfloat16)
    gate_weight_grad = jnp.dot(gate_grad.T, tokens, preferred_element_type=jnp.float32).astype(jnp.bfloat16)
    up_weight_grad = jnp.dot(up_grad.T, tokens, preferred_element_type=jnp.float32).astype(jnp.bfloat16)
    down_weight_grad = jnp.dot(hidden.T, upstream, preferred_element_type=jnp.float32).astype(jnp.bfloat16)
    return mixed, input_grad, gate_weight_grad, up_weight_grad, down_weight_grad
```

```python
import jax
import jax.numpy as jnp
from jax import lax
from jax.sharding import Mesh
from jax.sharding import PartitionSpec as P

AXES = ("z", "y", "x", "core", "tok")
BLK = ("z", "y", "x", "core")
PAIRS = ("tok", "core")
F32 = jnp.float32
BF16 = jnp.bfloat16


def shifted(block, axis, distance):
    count = lax.axis_size(axis)
    return lax.ppermute(block, axis, [(i, (i + distance) % count) for i in range(count)])


def gathered(block, axis, at):
    count = lax.axis_size(axis)
    return jnp.stack([block] + [shifted(block, axis, j) for j in range(1, count)], axis=at)


def reduced(blocks, axis):
    total = blocks[0].astype(F32)
    for j in range(1, len(blocks)):
        total = total + shifted(blocks[j], axis, -j).astype(F32)
    return total


def by_rows(left, right):
    return lax.dot_general(left, right, (((1,), (1,)), ((), ())), preferred_element_type=F32)


def by_columns(left, right):
    return lax.dot_general(left, right, (((0,), (0,)), ((), ())), preferred_element_type=F32)


def local(tokens, upstream, gate_weight, up_weight, down_weight):
    core = lax.axis_index("core")
    tok = lax.axis_index("tok")
    n_core, n_tok = lax.axis_size("core"), lax.axis_size("tok")
    width = tokens.shape[1]
    part = width // (n_core * n_tok)
    units = gate_weight.shape[0]
    own_at = (tok * n_core + core) * part
    other_at = (tok * n_core + 1 - core) * part

    mine = lax.all_to_all(
        jnp.stack([tokens, upstream]), PAIRS, split_axis=2, concat_axis=1, tiled=True
    )
    rows, grads = mine[0], mine[1]
    n = rows.shape[0]

    def at(weight, start):
        return lax.dynamic_slice_in_dim(weight, start, part, 1)

    sent = [at(w, other_at) for w in (gate_weight, up_weight, down_weight)]
    got = [shifted(w, "core", 1) for w in sent]
    own = [at(w, own_at) for w in (gate_weight, up_weight, down_weight)]
    in_weights = jnp.concatenate([own[0], own[1], got[0], got[1]], axis=0)
    out_weights = jnp.concatenate([own[2], got[2]], axis=0)

    grads = gathered(grads, "z", 0)
    rows = gathered(rows, "x", 0)
    grads = gathered(grads, "y", 0)
    rows = gathered(rows, "z", 0)
    grads = gathered(grads, "x", 2)
    rows = gathered(rows, "y", 0)
    n_y, n_z, n_x = rows.shape[:3]
    count = n_y * n_z * n_x * n
    rows = rows.reshape(count, part)
    grads = grads.reshape(count, part)

    out_part = by_rows(out_weights, grads)
    in_part = by_rows(in_weights, rows)
    hidden_grad = out_part[:units] + shifted(out_part[units:], "core", 1)
    gate_up = in_part[: 2 * units] + shifted(in_part[2 * units :], "core", 1)
    gate_up = gate_up + shifted(gate_up, "tok", 1)
    hidden_grad = hidden_grad + shifted(hidden_grad, "tok", 1)
    gate_value, up_value = gate_up[:units], gate_up[units:]

    gate_sigmoid = jax.nn.sigmoid(gate_value)
    swish_gate = gate_value * gate_sigmoid
    hidden = (swish_gate * up_value).astype(BF16)
    gate_grad = (
        hidden_grad * up_value * gate_sigmoid * (1.0 + gate_value * (1.0 - gate_sigmoid))
    ).astype(BF16)
    up_grad = (hidden_grad * swish_gate).astype(BF16)

    in_grads = jnp.concatenate([gate_grad, up_grad], axis=0)
    in_grads = jnp.concatenate([in_grads, shifted(in_grads, "core", 1)], axis=0)
    hidden = jnp.concatenate([hidden, shifted(hidden, "core", 1)], axis=0)

    input_part = by_columns(in_grads, in_weights).astype(BF16).reshape(n_y, n_z, n_x, n, part)
    input_part = reduced([input_part[:, :, j] for j in range(n_x)], "x").astype(BF16)
    step = count // n_y
    mixed_part = [
        by_columns(hidden[:, j * step : (j + 1) * step], out_weights).astype(BF16)
        for j in range(n_y)
    ]
    mixed_part = reduced(mixed_part, "y").astype(BF16).reshape(n_z, n_x, n, part)
    input_part = reduced([input_part[j] for j in range(n_y)], "y").astype(BF16)
    mixed_part = reduced([mixed_part[j] for j in range(n_z)], "z")
    input_part = reduced([input_part[j] for j in range(n_z)], "z")
    mixed_part = reduced([mixed_part[j] for j in range(n_x)], "x")
    summed = jnp.stack([mixed_part, input_part]).astype(BF16)
    summed = lax.all_to_all(summed, PAIRS, split_axis=1, concat_axis=2, tiled=True)

    in_weight_grad = jnp.dot(in_grads, rows, preferred_element_type=F32).astype(BF16)
    out_weight_grad = jnp.dot(hidden, grads, preferred_element_type=F32).astype(BF16)
    got_in = shifted(in_weight_grad[2 * units :], "core", 1)
    got_out = shifted(out_weight_grad[units:], "core", 1)

    def side_by_side(mine, others):
        first = jnp.where(core == 0, mine, others)
        second = jnp.where(core == 0, others, mine)
        return jnp.concatenate([first, second], axis=1)

    return (
        summed[0],
        summed[1],
        side_by_side(in_weight_grad[:units], got_in[:units]),
        side_by_side(in_weight_grad[units : 2 * units], got_in[units:]),
        side_by_side(out_weight_grad[:units], got_out),
    )


def solution(mesh):
    finer = Mesh(mesh.devices.reshape(8, 4, 2, 2, mesh.shape["tok"]), AXES)
    return jax.shard_map(
        local,
        mesh=finer,
        in_specs=(P(AXES, None), P(AXES, None), P(BLK, None), P(BLK, None), P(BLK, None)),
        out_specs=(P(AXES, None), P(AXES, None), P(BLK, "tok"), P(BLK, "tok"), P(BLK, "tok")),
        check_vma=False,
    )
```

```python
import functools

import jax
import jax.numpy as jnp
from jax import lax
from jax.experimental import pallas as pl
from jax.experimental.pallas import tpu as pltpu
from jax.sharding import Mesh
from jax.sharding import PartitionSpec as P

AXES = ("z", "y", "x", "core", "tok")
BLK = ("z", "y", "x", "core")
PLANE = ("y", "x")
PAIRS = ("tok", "core")
F32 = jnp.float32
BF16 = jnp.bfloat16
VMEM = pl.BlockSpec(memory_space=pltpu.VMEM)
SMEM = pl.BlockSpec(memory_space=pltpu.SMEM)
PARAMS = pltpu.CompilerParams(vmem_limit_bytes=40 * 1024 * 1024)


def shifted(block, axis, distance):
    count = lax.axis_size(axis)
    return lax.ppermute(block, axis, [(i, (i + distance) % count) for i in range(count)])


def exchanged(blocks, axes):
    return lax.all_to_all(blocks, axes, 0, 0, tiled=True)


def by_rows(left, right):
    return lax.dot_general(left, right, (((1,), (1,)), ((), ())), preferred_element_type=F32)


def by_columns(left, right):
    return lax.dot_general(left, right, (((0,), (0,)), ((), ())), preferred_element_type=F32)


def merge_kernel(first_ref, blocks_ref, out_ref, rows_ref, *, outer):
    per = blocks_ref.shape[0] // outer
    pair = blocks_ref.shape[1]
    for k in range(outer):
        member = lax.rem(first_ref[0] + k, outer)
        for q in range(per):
            at = (k * per + q) * pair
            rows_ref[at : at + pair, :] = blocks_ref[member * per + q].astype(F32)
    rows = rows_ref[...].astype(BF16)
    for j in range(out_ref.shape[0]):
        out_ref[j] = rows


def merged(blocks, first, outer, copies):
    n, pair, width = blocks.shape
    return pl.pallas_call(
        functools.partial(merge_kernel, outer=outer),
        out_shape=jax.ShapeDtypeStruct((copies, n * pair, width), BF16),
        in_specs=[SMEM, VMEM],
        out_specs=VMEM,
        scratch_shapes=[pltpu.VMEM((n * pair, width), F32)],
        compiler_params=PARAMS,
    )(first, blocks)


def split_kernel(first_ref, terms_ref, out_ref, rows_ref, *, outer):
    total = terms_ref[0].astype(F32)
    for j in range(1, terms_ref.shape[0]):
        total = total + terms_ref[j].astype(F32)
    rows_ref[...] = total
    per = out_ref.shape[0] // outer
    pair = out_ref.shape[1]
    for k in range(outer):
        member = lax.rem(first_ref[0] + k, outer)
        for q in range(per):
            at = (k * per + q) * pair
            out_ref[member * per + q] = rows_ref[at : at + pair, :].astype(BF16)


def split(terms, first, outer, pair):
    _, rows, width = terms.shape
    return pl.pallas_call(
        functools.partial(split_kernel, outer=outer),
        out_shape=jax.ShapeDtypeStruct((rows // pair, pair, width), BF16),
        in_specs=[SMEM, VMEM],
        out_specs=VMEM,
        scratch_shapes=[pltpu.VMEM((rows, width), F32)],
        compiler_params=PARAMS,
    )(first, terms)


def total_kernel(blocks_ref, out_ref, *, quarters):
    width = blocks_ref.shape[2]
    for q in range(quarters):
        total = blocks_ref[q].astype(F32)
        for j in range(1, blocks_ref.shape[0] // quarters):
            total = total + blocks_ref[j * quarters + q].astype(F32)
        out_ref[:, q * width : (q + 1) * width] = total.astype(BF16)


def totalled(blocks, quarters):
    n, pair, width = blocks.shape
    return pl.pallas_call(
        functools.partial(total_kernel, quarters=quarters),
        out_shape=jax.ShapeDtypeStruct((pair, quarters * width), BF16),
        in_specs=[VMEM],
        out_specs=VMEM,
        compiler_params=PARAMS,
    )(blocks)


def local(tokens, upstream, gate_weight, up_weight, down_weight):
    core = lax.axis_index("core")
    tok = lax.axis_index("tok")
    n_z = lax.axis_size("z")
    n_plane = lax.axis_size("y") * lax.axis_size("x")
    n_core = lax.axis_size("core")
    quarters = n_core * lax.axis_size("tok")
    pair, width = tokens.shape
    part = width // quarters
    units = gate_weight.shape[0]
    n = pair * quarters
    own_at = (tok * n_core + core) * part
    other_at = (tok * n_core + 1 - core) * part
    z_index = lax.axis_index("z").astype(jnp.int32).reshape(1)
    zero = jnp.zeros((1,), jnp.int32)

    def to_all(shard, copies):
        pieces = jnp.stack([shard[:, q * part : (q + 1) * part] for q in range(quarters)])
        return jnp.concatenate([pieces] * copies, axis=0)

    rows = exchanged(to_all(tokens, n_z), ("z", *PAIRS))
    rows = merged(rows, z_index, n_z, n_plane)
    grads = exchanged(to_all(upstream, n_plane), (*PLANE, *PAIRS))
    ring = [None] * n_z
    ring[0] = merged(grads, zero, n_plane, 1)[0]
    rows = exchanged(rows, PLANE)
    half = n_z // 2
    for k in range(1, half):
        ring[-k] = shifted(ring[1 - k], "z", 1)
        ring[k] = shifted(ring[k - 1], "z", -1)
    ring[half] = jnp.concatenate(
        [
            shifted(ring[half + 1][:, : part // 2], "z", 1),
            shifted(ring[half - 1][:, part // 2 :], "z", -1),
        ],
        axis=1,
    )
    count = n_plane * n_z * n
    rows = rows.reshape(count, part)
    grads = jnp.stack([r.reshape(n_plane, n, part) for r in ring], axis=1).reshape(count, part)

    def at(weight, start):
        return lax.dynamic_slice_in_dim(weight, start, part, 1)

    weights = (gate_weight, up_weight, down_weight)
    got = [shifted(at(w, other_at), "core", 1) for w in weights]
    own = [at(w, own_at) for w in weights]
    in_weights = jnp.concatenate([own[0], own[1], got[0], got[1]], axis=0)
    out_weights = jnp.concatenate([own[2], got[2]], axis=0)

    in_part = by_rows(in_weights, rows)
    gate_up = in_part[: 2 * units] + shifted(in_part[2 * units :], "core", 1)
    gate_up = gate_up + shifted(gate_up, "tok", 1)
    out_part = by_rows(out_weights, grads)
    hidden_grad = out_part[:units] + shifted(out_part[units:], "core", 1)
    hidden_grad = hidden_grad + shifted(hidden_grad, "tok", 1)
    gate_value, up_value = gate_up[:units], gate_up[units:]

    gate_sigmoid = jax.nn.sigmoid(gate_value)
    swish_gate = gate_value * gate_sigmoid
    hidden = (swish_gate * up_value).astype(BF16)
    gate_grad = (
        hidden_grad * up_value * gate_sigmoid * (1.0 + gate_value * (1.0 - gate_sigmoid))
    ).astype(BF16)
    up_grad = (hidden_grad * swish_gate).astype(BF16)

    in_grads = jnp.concatenate([gate_grad, up_grad], axis=0)
    in_grads = jnp.concatenate([in_grads, shifted(in_grads, "core", 1)], axis=0)
    hidden = jnp.concatenate([hidden, shifted(hidden, "core", 1)], axis=0)

    mixed_part = by_columns(hidden, out_weights).astype(BF16).reshape(n_plane, n_z * n, part)
    mixed = exchanged(mixed_part, PLANE)
    input_part = by_columns(in_grads, in_weights).reshape(n_plane, n_z, n, part)
    term = [input_part[:, k].reshape(n_plane * n, part) for k in range(n_z)]
    up = shifted(term[half][:, : part // 2].astype(BF16), "z", 1).astype(F32)
    down = shifted(term[half][:, part // 2 :].astype(BF16), "z", -1).astype(F32)
    up = jnp.concatenate([term[half - 1][:, : part // 2] + up, term[half - 1][:, part // 2 :]], 1)
    down = jnp.concatenate(
        [term[half + 1][:, : part // 2], term[half + 1][:, part // 2 :] + down], 1
    )
    for k in range(half - 2, -1, -1):
        up = shifted(up.astype(BF16), "z", 1).astype(F32)
        down = shifted(down.astype(BF16), "z", -1).astype(F32)
        if k:
            up, down = term[k] + up, term[-k] + down
    input_grad = split((term[0] + up + down)[None], zero, n_plane, pair)
    input_grad = totalled(exchanged(input_grad, (*PLANE, *PAIRS)), quarters)
    mixed = split(mixed, z_index, n_z, pair)
    mixed = totalled(exchanged(mixed, ("z", *PAIRS)), quarters)

    in_weight_grad = jnp.dot(in_grads, rows, preferred_element_type=F32).astype(BF16)
    out_weight_grad = jnp.dot(hidden, grads, preferred_element_type=F32).astype(BF16)
    got_in = shifted(in_weight_grad[2 * units :], "core", 1)
    got_out = shifted(out_weight_grad[units:], "core", 1)

    def side_by_side(mine, others):
        first = jnp.where(core == 0, mine, others)
        second = jnp.where(core == 0, others, mine)
        return jnp.concatenate([first, second], axis=1)

    return (
        mixed,
        input_grad,
        side_by_side(in_weight_grad[:units], got_in[:units]),
        side_by_side(in_weight_grad[units : 2 * units], got_in[units:]),
        side_by_side(out_weight_grad[:units], got_out),
    )


def solution(mesh):
    finer = Mesh(mesh.devices.reshape(8, 4, 2, 2, mesh.shape["tok"]), AXES)
    return jax.shard_map(
        local,
        mesh=finer,
        in_specs=(P(AXES, None), P(AXES, None), P(BLK, None), P(BLK, None), P(BLK, None)),
        out_specs=(P(AXES, None), P(AXES, None), P(BLK, "tok"), P(BLK, "tok"), P(BLK, "tok")),
        check_vma=False,
    )
```

```python
import functools

import jax
import jax.numpy as jnp
from jax import lax
from jax.experimental import pallas as pl
from jax.experimental.pallas import tpu as pltpu
from jax.sharding import Mesh
from jax.sharding import PartitionSpec as P

AXES = ("z", "y", "x", "core", "tok")
BLK = ("z", "y", "x", "core")
PLANE = ("y", "x")
PAIRS = ("tok", "core")
F32 = jnp.float32
BF16 = jnp.bfloat16
VMEM = pl.BlockSpec(memory_space=pltpu.VMEM)
SMEM = pl.BlockSpec(memory_space=pltpu.SMEM)
PARAMS = pltpu.CompilerParams(vmem_limit_bytes=40 * 1024 * 1024)


def shifted(block, axis, distance):
    count = lax.axis_size(axis)
    return lax.ppermute(block, axis, [(i, (i + distance) % count) for i in range(count)])


def exchanged(blocks, axes):
    return lax.all_to_all(blocks, axes, 0, 0, tiled=True)


def by_rows(left, right):
    return lax.dot_general(left, right, (((1,), (1,)), ((), ())), preferred_element_type=F32)


def by_columns(left, right):
    return lax.dot_general(left, right, (((0,), (0,)), ((), ())), preferred_element_type=F32)


def called(kernel, out_shape, *args, specs=None, scratch=(), **kwargs):
    specs = specs or [VMEM] * len(args)
    return pl.pallas_call(
        functools.partial(kernel, **kwargs),
        out_shape=out_shape,
        in_specs=specs,
        out_specs=jax.tree.map(lambda _: VMEM, out_shape),
        scratch_shapes=scratch,
        compiler_params=PARAMS,
    )(*args)


def called_at(kernel, out_shape, places, *args, index=None, scratch=(), **kwargs):
    def whole(shape):
        return pl.BlockSpec(shape, lambda *_: (0,) * len(shape))

    specs = [
        whole(arg.shape) if place is None else pl.BlockSpec(*place)
        for arg, place in zip(args, places, strict=True)
    ]
    grid = pltpu.PrefetchScalarGridSpec(
        num_scalar_prefetch=1,
        grid=(1,),
        in_specs=specs,
        out_specs=jax.tree.map(lambda o: whole(o.shape), out_shape),
        scratch_shapes=scratch,
    )
    return pl.pallas_call(
        functools.partial(kernel, **kwargs),
        out_shape=out_shape,
        grid_spec=grid,
        compiler_params=PARAMS,
    )(jnp.zeros((1,), jnp.int32) if index is None else index, *args)


def shape_of(shape, kind=BF16):
    return jax.ShapeDtypeStruct(shape, kind)


def deal_kernel(tokens_ref, upstream_ref, first_ref, second_ref, *, quarters):
    part = tokens_ref.shape[1] // quarters
    for q in range(quarters):
        rows = tokens_ref[:, q * part : (q + 1) * part]
        grads = upstream_ref[:, q * part : (q + 1) * part]
        for j in range(first_ref.shape[0] // quarters):
            first_ref[j * quarters + q] = rows
        for j in range(second_ref.shape[0] // quarters):
            second_ref[j * quarters + q] = grads


def merge_kernel(blocks_ref, out_ref, rows_ref):
    n, pair, _ = blocks_ref.shape
    for j in range(n):
        rows_ref[j * pair : (j + 1) * pair, :] = blocks_ref[j].astype(F32)
    out_ref[...] = rows_ref[...].astype(BF16)


def merge_from_kernel(first_ref, blocks_ref, out_ref, rows_ref, *, outer):
    n, pair, _ = blocks_ref.shape
    per = n // outer
    for k in range(outer):
        member = lax.rem(first_ref[0] + k, outer)
        for q in range(per):
            at = (k * per + q) * pair
            rows_ref[at : at + pair, :] = blocks_ref[member * per + q].astype(F32)
    rows = rows_ref[...].astype(BF16)
    for j in range(out_ref.shape[0]):
        out_ref[j] = rows


def stack_kernel(*refs, place):
    *block_refs, left_ref, right_ref, out_ref = refs
    height = left_ref.shape[0]
    middle = left_ref.shape[1]
    places = [k for k in range(len(block_refs) + 1) if k != place]
    for k, block_ref in zip(places, block_refs, strict=True):
        out_ref[k * height : (k + 1) * height, :] = block_ref[...]
    out_ref[place * height : (place + 1) * height, :middle] = left_ref[...]
    out_ref[place * height : (place + 1) * height, middle:] = right_ref[...]


def pack_kernel(_, gate_ref, up_ref, down_ref, out_ref):
    units = gate_ref.shape[0]
    for j, ref in enumerate((gate_ref, up_ref, down_ref)):
        out_ref[j * units : (j + 1) * units, :] = ref[...]


def weights_kernel(_, gate_ref, up_ref, down_ref, got_ref, in_ref, out_ref):
    units = gate_ref.shape[0]
    in_ref[:units, :] = gate_ref[...]
    in_ref[units : 2 * units, :] = up_ref[...]
    in_ref[2 * units :, :] = got_ref[: 2 * units, :]
    out_ref[:units, :] = down_ref[...]
    out_ref[units:, :] = got_ref[2 * units :, :]


def middle_kernel(sum_ref, got_ref, hid_ref, hid_got_ref, out_ref):
    units = hid_ref.shape[0]
    gate_value = sum_ref[:units, :] + got_ref[:units, :]
    up_value = sum_ref[units:, :] + got_ref[units:, :]
    hidden_grad = hid_ref[...] + hid_got_ref[...]
    gate_sigmoid = jax.nn.sigmoid(gate_value)
    swish_gate = gate_value * gate_sigmoid
    gate_grad = hidden_grad * up_value * gate_sigmoid * (1.0 + gate_value * (1.0 - gate_sigmoid))
    out_ref[:units, :] = gate_grad.astype(BF16)
    out_ref[units : 2 * units, :] = (hidden_grad * swish_gate).astype(BF16)
    out_ref[2 * units :, :] = (swish_gate * up_value).astype(BF16)


def pair_kernel(own_ref, got_ref, in_ref, hidden_ref):
    double = in_ref.shape[0] // 2
    in_ref[:double, :] = own_ref[:double, :]
    in_ref[double:, :] = got_ref[:double, :]
    hidden_ref[: double // 2, :] = own_ref[double:, :]
    hidden_ref[double // 2 :, :] = got_ref[double:, :]


def both_of(left_ref, right_ref):
    return jnp.concatenate([left_ref[...], right_ref[...]], axis=1)


def open_kernel(_, left_ref, right_ref, up_ref, down_ref):
    term = both_of(left_ref, right_ref)
    middle = up_ref.shape[1]
    up_ref[...] = term[:, :middle].astype(BF16)
    down_ref[...] = term[:, middle:].astype(BF16)


def turn_kernel(_, la_ref, ra_ref, lb_ref, rb_ref, came_up_ref, came_down_ref, up_ref, down_ref):
    ahead, behind = both_of(la_ref, ra_ref), both_of(lb_ref, rb_ref)
    reach = came_up_ref.shape[1]
    width = up_ref.shape[1]
    start = width - came_down_ref.shape[1]
    up_ref[:, :reach] = (ahead[:, :reach] + came_up_ref[...].astype(F32)).astype(BF16)
    if reach < width:
        up_ref[:, reach:] = ahead[:, reach:].astype(BF16)
        down_ref[:, :start] = behind[:, :start].astype(BF16)
    down_ref[:, start:] = (behind[:, start:] + came_down_ref[...].astype(F32)).astype(BF16)


def close_kernel(_, left_ref, right_ref, came_up_ref, came_down_ref, out_ref, rows_ref):
    n, pair, _ = out_ref.shape
    total = both_of(left_ref, right_ref)
    total = total + came_up_ref[...].astype(F32) + came_down_ref[...].astype(F32)
    rows_ref[...] = total
    for j in range(n):
        out_ref[j] = rows_ref[j * pair : (j + 1) * pair, :].astype(BF16)


def split_from_kernel(first_ref, terms_ref, out_ref, rows_ref, *, outer):
    n, pair, _ = out_ref.shape
    per = n // outer
    total = terms_ref[0].astype(F32)
    for j in range(1, terms_ref.shape[0]):
        total = total + terms_ref[j].astype(F32)
    rows_ref[...] = total
    for k in range(outer):
        member = lax.rem(first_ref[0] + k, outer)
        for q in range(per):
            at = (k * per + q) * pair
            out_ref[member * per + q] = rows_ref[at : at + pair, :].astype(BF16)


def total_kernel(first_ref, second_ref, mixed_ref, input_ref, *, quarters):
    part = input_ref.shape[1] // quarters
    cut = first_ref.shape[2] - part

    def summed(ref, q):
        total = ref[q].astype(F32)
        for j in range(1, ref.shape[0] // quarters):
            total = total + ref[j * quarters + q].astype(F32)
        return total.astype(BF16)

    for q in range(quarters):
        at = q * part
        total = summed(first_ref, q)
        input_ref[:, at : at + part] = total[:, :part]
        mixed_ref[:, at : at + cut] = total[:, part:]
        mixed_ref[:, at + cut : at + part] = summed(second_ref, q)


def ring_reduced(left, right, count, pair):
    height = left.shape[0] // count
    width = left.shape[1] + right.shape[1]
    half, middle = count // 2, width // 256 * 128

    def at(k):
        return [
            ((height, a.shape[1]), functools.partial(lambda k, *_: (k, 0), k)) for a in (left, right)
        ]

    up, down = called_at(
        open_kernel,
        (shape_of((height, middle)), shape_of((height, width - middle))),
        at(half),
        left,
        right,
    )
    for k in range(half - 1, 0, -1):
        up, down = shifted(up, "z", 1), shifted(down, "z", -1)
        up, down = called_at(
            turn_kernel,
            (shape_of((height, width)), shape_of((height, width))),
            [*at(k), *at(count - k), None, None],
            left,
            right,
            left,
            right,
            up,
            down,
        )
    up, down = shifted(up, "z", 1), shifted(down, "z", -1)
    return called_at(
        close_kernel,
        shape_of((height // pair, pair, width)),
        [*at(0), None, None],
        left,
        right,
        up,
        down,
        scratch=[pltpu.VMEM((height, width), F32)],
    )


def local(tokens, upstream, gate_weight, up_weight, down_weight):
    core = lax.axis_index("core")
    tok = lax.axis_index("tok")
    n_z = lax.axis_size("z")
    n_plane = lax.axis_size("y") * lax.axis_size("x")
    n_core = lax.axis_size("core")
    quarters = n_core * lax.axis_size("tok")
    pair, width = tokens.shape
    part = width // quarters
    cut = part // 8 * 3
    units = gate_weight.shape[0]
    n = pair * quarters
    n_line, n_rows = n_z * n, n_plane * n
    count = n_z * n_plane * n
    own_at = (tok * n_core + core).astype(jnp.int32).reshape(1)
    other_at = (tok * n_core + 1 - core).astype(jnp.int32).reshape(1)
    z_index = lax.axis_index("z").astype(jnp.int32).reshape(1)

    first, second = called(
        deal_kernel,
        (
            shape_of((n_plane * quarters, pair, part)),
            shape_of((n_z * quarters, pair, part)),
        ),
        tokens,
        upstream,
        quarters=quarters,
    )
    weights = (gate_weight, up_weight, down_weight)
    column = ((units, part), lambda i, at: (0, at[0]))
    sent = called_at(pack_kernel, shape_of((3 * units, part)), [column] * 3, *weights, index=other_at)
    got = shifted(sent, "core", 1)
    first = exchanged(first, (*PLANE, *PAIRS))
    rows = called(
        merge_kernel, shape_of((n_rows, part)), first, scratch=[pltpu.VMEM((n_rows, part), F32)]
    )
    rows, second = lax.optimization_barrier((rows, second))
    half, middle = n_z // 2, part // 2
    ring = [rows] + [None] * (n_z - 1)
    for k in range(1, half):
        ring[k] = shifted(ring[k - 1], "z", -1)
        ring[-k] = shifted(ring[1 - k], "z", 1)
        if k == 1:
            in_weights, out_weights = called_at(
                weights_kernel,
                (shape_of((4 * units, part)), shape_of((2 * units, part))),
                [column] * 3 + [None],
                *weights,
                got,
                index=own_at,
            )
            ring[1], in_weights, out_weights = lax.optimization_barrier(
                (ring[1], in_weights, out_weights)
            )
    rows = called(
        stack_kernel,
        shape_of((count, part)),
        *(block for k, block in enumerate(ring) if k != half),
        shifted(ring[half - 1][:, :middle], "z", -1),
        shifted(ring[half + 1][:, middle:], "z", 1),
        place=half,
    )
    grads = called(
        merge_from_kernel,
        shape_of((n_plane, n_line, part)),
        z_index,
        exchanged(second, ("z", *PAIRS)),
        specs=[SMEM, VMEM],
        scratch=[pltpu.VMEM((n_line, part), F32)],
        outer=n_z,
    )
    grads = exchanged(grads, PLANE).reshape(n_plane, n_z, n, part)
    grads = grads.swapaxes(0, 1).reshape(count, part)

    gate_up = shifted(by_rows(in_weights[2 * units :], rows), "core", 1)
    gate_up = by_rows(in_weights[: 2 * units], rows) + gate_up
    hidden_grad = shifted(by_rows(out_weights[units:], grads), "core", 1)
    hidden_grad = by_rows(out_weights[:units], grads) + hidden_grad
    own = called(
        middle_kernel,
        shape_of((3 * units, count)),
        gate_up,
        shifted(gate_up, "tok", 1),
        hidden_grad,
        shifted(hidden_grad, "tok", 1),
    )
    in_grads, hidden = called(
        pair_kernel,
        (shape_of((4 * units, count)), shape_of((2 * units, count))),
        own,
        shifted(own, "core", 1),
    )

    rest = by_columns(hidden, out_weights[:, cut:]).astype(BF16)
    rest = rest.reshape(n_z, n_plane, n, part - cut).swapaxes(0, 1)
    rest = rest.reshape(n_plane, n_line, part - cut)
    rest, in_grads, hidden = lax.optimization_barrier((rest, in_grads, hidden))
    rest = called(
        split_from_kernel,
        shape_of((n_z * quarters, pair, part - cut)),
        z_index,
        exchanged(rest, PLANE),
        specs=[SMEM, VMEM],
        scratch=[pltpu.VMEM((n_line, part - cut), F32)],
        outer=n_z,
    )
    rest = exchanged(rest, ("z", *PAIRS))
    summed = ring_reduced(
        by_columns(in_grads, in_weights), by_columns(hidden, out_weights[:, :cut]), n_z, pair
    )
    summed, rest = lax.optimization_barrier((summed, rest))
    mixed, input_grad = called(
        total_kernel,
        (shape_of((pair, width)), shape_of((pair, width))),
        exchanged(summed, (*PLANE, *PAIRS)),
        rest,
        quarters=quarters,
    )

    def product(left, right):
        return jnp.dot(left, right, preferred_element_type=F32).astype(BF16)

    got_in = shifted(product(in_grads[2 * units :], rows), "core", 1)
    got_out = shifted(product(hidden[units:], grads), "core", 1)
    in_weight_grad = product(in_grads[: 2 * units], rows)
    out_weight_grad = product(hidden[:units], grads)

    def side_by_side(mine, others):
        left = jnp.where(core == 0, mine, others)
        right = jnp.where(core == 0, others, mine)
        return jnp.concatenate([left, right], axis=1)

    return (
        mixed,
        input_grad,
        side_by_side(in_weight_grad[:units], got_in[:units]),
        side_by_side(in_weight_grad[units:], got_in[units:]),
        side_by_side(out_weight_grad, got_out),
    )


def solution(mesh):
    finer = Mesh(mesh.devices.reshape(8, 4, 2, 2, mesh.shape["tok"]), AXES)
    return jax.shard_map(
        local,
        mesh=finer,
        in_specs=(P(AXES, None), P(AXES, None), P(BLK, None), P(BLK, None), P(BLK, None)),
        out_specs=(P(AXES, None), P(AXES, None), P(BLK, "tok"), P(BLK, "tok"), P(BLK, "tok")),
        check_vma=False,
    )
```

```python
import functools

import jax
import jax.numpy as jnp
from jax import lax
from jax.experimental import pallas as pl
from jax.experimental.pallas import tpu as pltpu
from jax.sharding import Mesh
from jax.sharding import PartitionSpec as P

AXES = ("z", "y", "x", "core", "tok")
BLK = ("z", "y", "x", "core")
PLANE = ("y", "x")
PAIRS = ("tok", "core")
F32 = jnp.float32
BF16 = jnp.bfloat16
VMEM = pl.BlockSpec(memory_space=pltpu.VMEM)
SMEM = pl.BlockSpec(memory_space=pltpu.SMEM)
PARAMS = pltpu.CompilerParams(vmem_limit_bytes=20 * 1024 * 1024)
LARGE = pltpu.CompilerParams(vmem_limit_bytes=58 * 1024 * 1024)


def shifted(block, axis, distance):
    count = lax.axis_size(axis)
    return lax.ppermute(block, axis, [(i, (i + distance) % count) for i in range(count)])


def exchanged(blocks, axes):
    return lax.all_to_all(blocks, axes, 0, 0, tiled=True)


def by_rows(left, right):
    return lax.dot_general(left, right, (((1,), (1,)), ((), ())), preferred_element_type=F32)


def by_columns(left, right):
    return lax.dot_general(left, right, (((0,), (0,)), ((), ())), preferred_element_type=F32)


def called(kernel, out_shape, *args, specs=None, scratch=(), params=PARAMS, **kwargs):
    specs = specs or [VMEM] * len(args)
    return pl.pallas_call(
        functools.partial(kernel, **kwargs),
        out_shape=out_shape,
        in_specs=specs,
        out_specs=jax.tree.map(lambda _: VMEM, out_shape),
        scratch_shapes=scratch,
        compiler_params=params,
    )(*args)


def called_at(kernel, out_shape, places, *args, index=None, scratch=(), params=PARAMS, **kwargs):
    def whole(shape):
        return pl.BlockSpec(shape, lambda *_: (0,) * len(shape))

    specs = [
        whole(arg.shape) if place is None else pl.BlockSpec(*place)
        for arg, place in zip(args, places, strict=True)
    ]
    grid = pltpu.PrefetchScalarGridSpec(
        num_scalar_prefetch=1,
        grid=(1,),
        in_specs=specs,
        out_specs=jax.tree.map(lambda o: whole(o.shape), out_shape),
        scratch_shapes=scratch,
    )
    return pl.pallas_call(
        functools.partial(kernel, **kwargs),
        out_shape=out_shape,
        grid_spec=grid,
        compiler_params=params,
    )(jnp.zeros((1,), jnp.int32) if index is None else index, *args)


def shape_of(shape, kind=BF16):
    return jax.ShapeDtypeStruct(shape, kind)


def deal_kernel(tokens_ref, upstream_ref, first_ref, second_ref, *, quarters):
    part = tokens_ref.shape[1] // quarters
    cut = first_ref.shape[2] - part
    for q in range(quarters):
        at = q * part
        rows = tokens_ref[:, at : at + part]
        grads = upstream_ref[:, at : at + cut]
        rest = upstream_ref[:, at + cut : at + part]
        for j in range(first_ref.shape[0] // quarters):
            first_ref[j * quarters + q, :, :part] = rows
            first_ref[j * quarters + q, :, part:] = grads
        for j in range(second_ref.shape[0] // quarters):
            second_ref[j * quarters + q] = rest


def merge_kernel(blocks_ref, out_ref, rows_ref):
    n, pair, _ = blocks_ref.shape
    for j in range(n):
        rows_ref[j * pair : (j + 1) * pair, :] = blocks_ref[j].astype(F32)
    out_ref[...] = rows_ref[...].astype(BF16)


def merge_from_kernel(first_ref, blocks_ref, out_ref, rows_ref, *, outer):
    n, pair, _ = blocks_ref.shape
    per = n // outer
    for k in range(outer):
        member = lax.rem(first_ref[0] + k, outer)
        for q in range(per):
            at = (k * per + q) * pair
            rows_ref[at : at + pair, :] = blocks_ref[member * per + q].astype(F32)
    rows = rows_ref[...].astype(BF16)
    for j in range(out_ref.shape[0]):
        out_ref[j] = rows


def stack_kernel(*refs, place, n):
    *block_refs, left_ref, right_ref, rest_ref, rows_ref, grads_ref = refs
    height, middle = left_ref.shape
    part = rows_ref.shape[1]
    cut = block_refs[0].shape[1] - part
    places = [k for k in range(len(block_refs) + 1) if k != place]
    for k, block_ref in zip(places, block_refs, strict=True):
        at = slice(k * height, (k + 1) * height)
        rows_ref[at, :] = block_ref[:, :part]
        grads_ref[at, :cut] = block_ref[:, part:]
    at = slice(place * height, (place + 1) * height)
    rows_ref[at, :middle] = left_ref[...]
    rows_ref[at, middle:] = right_ref[:, : part - middle]
    grads_ref[at, :cut] = right_ref[:, part - middle :]
    for k in range(len(block_refs) + 1):
        for j in range(rest_ref.shape[0]):
            at = k * height + j * n
            grads_ref[at : at + n, cut:] = rest_ref[j, k * n : (k + 1) * n, :]


def pack_kernel(_, gate_ref, up_ref, down_ref, out_ref):
    units = gate_ref.shape[0]
    for j, ref in enumerate((gate_ref, up_ref, down_ref)):
        out_ref[j * units : (j + 1) * units, :] = ref[...]


def weights_kernel(_, gate_ref, up_ref, down_ref, got_ref, in_ref, out_ref):
    units = gate_ref.shape[0]
    in_ref[:units, :] = gate_ref[...]
    in_ref[units : 2 * units, :] = up_ref[...]
    in_ref[2 * units :, :] = got_ref[: 2 * units, :]
    out_ref[:units, :] = down_ref[...]
    out_ref[units:, :] = got_ref[2 * units :, :]


def middle_kernel(sum_ref, got_ref, hid_ref, hid_got_ref, out_ref):
    units = hid_ref.shape[0]
    gate_value = sum_ref[:units, :] + got_ref[:units, :].astype(F32)
    up_value = sum_ref[units:, :] + got_ref[units:, :].astype(F32)
    hidden_grad = hid_ref[...] + hid_got_ref[...].astype(F32)
    gate_sigmoid = jax.nn.sigmoid(gate_value)
    swish_gate = gate_value * gate_sigmoid
    gate_grad = hidden_grad * up_value * gate_sigmoid * (1.0 + gate_value * (1.0 - gate_sigmoid))
    out_ref[:units, :] = gate_grad.astype(BF16)
    out_ref[units : 2 * units, :] = (hidden_grad * swish_gate).astype(BF16)
    out_ref[2 * units :, :] = (swish_gate * up_value).astype(BF16)


def pair_kernel(own_ref, got_ref, in_ref, hidden_ref):
    double = in_ref.shape[0] // 2
    in_ref[:double, :] = own_ref[:double, :]
    in_ref[double:, :] = got_ref[:double, :]
    hidden_ref[: double // 2, :] = own_ref[double:, :]
    hidden_ref[double // 2 :, :] = got_ref[double:, :]


def both_of(left_ref, right_ref):
    return jnp.concatenate([left_ref[...], right_ref[...]], axis=1)


def open_kernel(_, left_ref, right_ref, up_ref, down_ref):
    term = both_of(left_ref, right_ref)
    middle = up_ref.shape[1]
    up_ref[...] = term[:, :middle].astype(BF16)
    down_ref[...] = term[:, middle:].astype(BF16)


def turn_kernel(_, la_ref, ra_ref, lb_ref, rb_ref, came_up_ref, came_down_ref, up_ref, down_ref):
    ahead, behind = both_of(la_ref, ra_ref), both_of(lb_ref, rb_ref)
    reach = came_up_ref.shape[1]
    width = up_ref.shape[1]
    start = width - came_down_ref.shape[1]
    up_ref[:, :reach] = (ahead[:, :reach] + came_up_ref[...].astype(F32)).astype(BF16)
    if reach < width:
        up_ref[:, reach:] = ahead[:, reach:].astype(BF16)
        down_ref[:, :start] = behind[:, :start].astype(BF16)
    down_ref[:, start:] = (behind[:, start:] + came_down_ref[...].astype(F32)).astype(BF16)


def close_kernel(_, left_ref, right_ref, came_up_ref, came_down_ref, out_ref, rows_ref):
    n, pair, _ = out_ref.shape
    total = both_of(left_ref, right_ref)
    total = total + came_up_ref[...].astype(F32) + came_down_ref[...].astype(F32)
    rows_ref[...] = total
    for j in range(n):
        out_ref[j] = rows_ref[j * pair : (j + 1) * pair, :].astype(BF16)


def split_from_kernel(first_ref, terms_ref, out_ref, rows_ref, *, outer):
    n, pair, _ = out_ref.shape
    per = n // outer
    total = terms_ref[0].astype(F32)
    for j in range(1, terms_ref.shape[0]):
        total = total + terms_ref[j].astype(F32)
    rows_ref[...] = total
    for k in range(outer):
        member = lax.rem(first_ref[0] + k, outer)
        for q in range(per):
            at = (k * per + q) * pair
            out_ref[member * per + q] = rows_ref[at : at + pair, :].astype(BF16)


def total_kernel(first_ref, second_ref, mixed_ref, input_ref, *, quarters):
    part = mixed_ref.shape[1] // quarters
    cut = first_ref.shape[2] - part

    def summed(ref, q):
        total = ref[q].astype(F32)
        for j in range(1, ref.shape[0] // quarters):
            total = total + ref[j * quarters + q].astype(F32)
        return total.astype(BF16)

    for q in range(quarters):
        at = q * part
        total = summed(first_ref, q)
        mixed_ref[:, at : at + part] = total[:, :part]
        input_ref[:, at : at + cut] = total[:, part:]
        input_ref[:, at + cut : at + part] = summed(second_ref, q)


def ring_reduced(left, right, count, pair, beside):
    height = left.shape[0] // count
    width = left.shape[1] + right.shape[1]
    half, middle = count // 2, width // 256 * 128

    def at(k):
        return [
            ((height, a.shape[1]), functools.partial(lambda k, *_: (k, 0), k)) for a in (left, right)
        ]

    up, down = called_at(
        open_kernel,
        (shape_of((height, middle)), shape_of((height, width - middle))),
        at(half),
        left,
        right,
    )
    for k in range(half - 1, 0, -1):
        up, down = shifted(up, "z", 1), shifted(down, "z", -1)
        if k == 1:
            up, down, beside = lax.optimization_barrier((up, down, beside))
        up, down = called_at(
            turn_kernel,
            (shape_of((height, width)), shape_of((height, width))),
            [*at(k), *at(count - k), None, None],
            left,
            right,
            left,
            right,
            up,
            down,
        )
    up, down = shifted(up, "z", 1), shifted(down, "z", -1)
    summed = called_at(
        close_kernel,
        shape_of((height // pair, pair, width)),
        [*at(0), None, None],
        left,
        right,
        up,
        down,
        scratch=[pltpu.VMEM((height, width), F32)],
    )
    return summed, beside


def local(tokens, upstream, gate_weight, up_weight, down_weight):
    core = lax.axis_index("core")
    tok = lax.axis_index("tok")
    n_z = lax.axis_size("z")
    n_plane = lax.axis_size("y") * lax.axis_size("x")
    n_core = lax.axis_size("core")
    quarters = n_core * lax.axis_size("tok")
    pair, width = tokens.shape
    part = width // quarters
    cut = part // 8 * 4
    turn = part // 8 * 3
    units = gate_weight.shape[0]
    n = pair * quarters
    n_line, n_rows = n_z * n, n_plane * n
    count = n_z * n_plane * n
    own_at = (tok * n_core + core).astype(jnp.int32).reshape(1)
    other_at = (tok * n_core + 1 - core).astype(jnp.int32).reshape(1)
    z_index = lax.axis_index("z").astype(jnp.int32).reshape(1)

    first, second = called(
        deal_kernel,
        (
            shape_of((n_plane * quarters, pair, part + cut)),
            shape_of((n_z * quarters, pair, part - cut)),
        ),
        tokens,
        upstream,
        quarters=quarters,
    )
    first, *weights = lax.optimization_barrier((first, gate_weight, up_weight, down_weight))
    column = ((units, part), lambda i, at: (0, at[0]))
    sent = called_at(pack_kernel, shape_of((3 * units, part)), [column] * 3, *weights, index=other_at, params=LARGE)
    got = shifted(sent, "core", 1)
    first = exchanged(first, (*PLANE, *PAIRS))
    in_weights, out_weights = called_at(
        weights_kernel,
        (shape_of((4 * units, part)), shape_of((2 * units, part))),
        [column] * 3 + [None],
        *weights,
        got,
        index=own_at,
        params=LARGE,
    )
    first, in_weights, out_weights = lax.optimization_barrier((first, in_weights, out_weights))
    rows = called(
        merge_kernel,
        shape_of((n_rows, part + cut)),
        first,
        scratch=[pltpu.VMEM((n_rows, part + cut), F32)],
    )
    rows, second = lax.optimization_barrier((rows, second))
    half, middle = n_z // 2, (part + cut) // 256 * 128
    ring = [rows] + [None] * (n_z - 1)
    for k in range(1, half):
        ring[k] = shifted(ring[k - 1], "z", -1)
        ring[-k] = shifted(ring[1 - k], "z", 1)
    rest = called(
        merge_from_kernel,
        shape_of((n_plane, n_line, part - cut)),
        z_index,
        exchanged(second, ("z", *PAIRS)),
        specs=[SMEM, VMEM],
        scratch=[pltpu.VMEM((n_line, part - cut), F32)],
        outer=n_z,
    )
    rest = exchanged(rest, PLANE)
    rows, grads = called(
        stack_kernel,
        (shape_of((count, part)), shape_of((count, part))),
        *(block for k, block in enumerate(ring) if k != half),
        shifted(ring[half - 1][:, :middle], "z", -1),
        shifted(ring[half + 1][:, middle:], "z", 1),
        rest,
        place=half,
        n=n,
        params=LARGE,
    )

    gate_up = shifted(by_rows(in_weights[2 * units :], rows), "core", 1)
    gate_up = by_rows(in_weights[: 2 * units], rows) + gate_up
    hidden_grad = shifted(by_rows(out_weights[units:], grads), "core", 1)
    hidden_grad = by_rows(out_weights[:units], grads) + hidden_grad
    own = called(
        middle_kernel,
        shape_of((3 * units, count)),
        gate_up,
        shifted(gate_up.astype(BF16), "tok", 1),
        hidden_grad,
        shifted(hidden_grad.astype(BF16), "tok", 1),
    )
    in_grads, hidden = called(
        pair_kernel,
        (shape_of((4 * units, count)), shape_of((2 * units, count))),
        own,
        shifted(own, "core", 1),
    )

    rest = by_columns(in_grads, in_weights[:, turn:]).astype(BF16)
    rest = rest.reshape(n_z, n_plane, n, part - turn).swapaxes(0, 1)
    rest = rest.reshape(n_plane, n_line, part - turn)
    rest, in_grads, hidden = lax.optimization_barrier((rest, in_grads, hidden))
    rest = called(
        split_from_kernel,
        shape_of((n_z * quarters, pair, part - turn)),
        z_index,
        exchanged(rest, PLANE),
        specs=[SMEM, VMEM],
        scratch=[pltpu.VMEM((n_line, part - turn), F32)],
        outer=n_z,
    )
    summed, rest = ring_reduced(
        by_columns(hidden, out_weights),
        by_columns(in_grads, in_weights[:, :turn]),
        n_z,
        pair,
        rest,
    )
    rest = exchanged(rest, ("z", *PAIRS))
    summed, rest = lax.optimization_barrier((summed, rest))
    mixed, input_grad = called(
        total_kernel,
        (shape_of((pair, width)), shape_of((pair, width))),
        exchanged(summed, (*PLANE, *PAIRS)),
        rest,
        quarters=quarters,
    )

    def product(left, right):
        return jnp.dot(left, right, preferred_element_type=F32).astype(BF16)

    got_in = shifted(product(in_grads[2 * units :], rows), "core", 1)
    got_out = shifted(product(hidden[units:], grads), "core", 1)
    in_weight_grad = product(in_grads[: 2 * units], rows)
    out_weight_grad = product(hidden[:units], grads)

    def side_by_side(mine, others):
        left = jnp.where(core == 0, mine, others)
        right = jnp.where(core == 0, others, mine)
        return jnp.concatenate([left, right], axis=1)

    return (
        mixed,
        input_grad,
        side_by_side(in_weight_grad[:units], got_in[:units]),
        side_by_side(in_weight_grad[units:], got_in[units:]),
        side_by_side(out_weight_grad, got_out),
    )


def solution(mesh):
    finer = Mesh(mesh.devices.reshape(8, 4, 2, 2, mesh.shape["tok"]), AXES)
    return jax.shard_map(
        local,
        mesh=finer,
        in_specs=(P(AXES, None), P(AXES, None), P(BLK, None), P(BLK, None), P(BLK, None)),
        out_specs=(P(AXES, None), P(AXES, None), P(BLK, "tok"), P(BLK, "tok"), P(BLK, "tok")),
        check_vma=False,
    )
```

```python
import functools

import jax
import jax.numpy as jnp
from jax import lax
from jax.experimental import pallas as pl
from jax.experimental.pallas import tpu as pltpu
from jax.sharding import Mesh
from jax.sharding import PartitionSpec as P

AXES = ("z", "y", "x", "core", "tok")
BLK = ("z", "y", "x", "core")
PLANE = ("y", "x")
PAIRS = ("tok", "core")
F32 = jnp.float32
BF16 = jnp.bfloat16
VMEM = pl.BlockSpec(memory_space=pltpu.VMEM)
SMEM = pl.BlockSpec(memory_space=pltpu.SMEM)
ANY = pl.BlockSpec(memory_space=pl.ANY)
PARAMS = pltpu.CompilerParams(vmem_limit_bytes=20 * 1024 * 1024)
LARGE = pltpu.CompilerParams(vmem_limit_bytes=58 * 1024 * 1024)


def shifted(block, axis, distance):
    count = lax.axis_size(axis)
    return lax.ppermute(block, axis, [(i, (i + distance) % count) for i in range(count)])


def exchanged(blocks, axes):
    return lax.all_to_all(blocks, axes, 0, 0, tiled=True)


def by_rows(left, right):
    return lax.dot_general(left, right, (((1,), (1,)), ((), ())), preferred_element_type=F32)


def by_columns(left, right):
    return lax.dot_general(left, right, (((0,), (0,)), ((), ())), preferred_element_type=F32)


def called(kernel, out_shape, *args, specs=None, scratch=(), **kwargs):
    specs = specs or [VMEM] * len(args)
    return pl.pallas_call(
        functools.partial(kernel, **kwargs),
        out_shape=out_shape,
        in_specs=specs,
        out_specs=jax.tree.map(lambda _: VMEM, out_shape),
        scratch_shapes=scratch,
        compiler_params=PARAMS,
    )(*args)


def called_at(kernel, out_shape, places, *args, index=None, scratch=(), **kwargs):
    def whole(shape):
        return pl.BlockSpec(shape, lambda *_: (0,) * len(shape))

    specs = [
        whole(arg.shape) if place is None else pl.BlockSpec(*place)
        for arg, place in zip(args, places, strict=True)
    ]
    grid = pltpu.PrefetchScalarGridSpec(
        num_scalar_prefetch=1,
        grid=(1,),
        in_specs=specs,
        out_specs=jax.tree.map(lambda o: whole(o.shape), out_shape),
        scratch_shapes=scratch,
    )
    return pl.pallas_call(
        functools.partial(kernel, **kwargs),
        out_shape=out_shape,
        grid_spec=grid,
        compiler_params=PARAMS,
    )(jnp.zeros((1,), jnp.int32) if index is None else index, *args)


def shape_of(shape, kind=BF16):
    return jax.ShapeDtypeStruct(shape, kind)


def deal_kernel(tokens_ref, upstream_ref, out_ref, *, quarters):
    part = tokens_ref.shape[1] // quarters
    for q in range(quarters):
        rows = tokens_ref[:, q * part : (q + 1) * part]
        grads = upstream_ref[:, q * part : (q + 1) * part]
        for j in range(out_ref.shape[0] // quarters):
            out_ref[j * quarters + q, :, :part] = rows
            out_ref[j * quarters + q, :, part:] = grads


def merge_kernel(blocks_ref, left_ref, right_ref, rows_ref):
    n, pair, _ = blocks_ref.shape
    for j in range(n):
        rows_ref[j * pair : (j + 1) * pair, :] = blocks_ref[j].astype(F32)
    left_ref[...] = rows_ref[:, : left_ref.shape[1]].astype(BF16)
    right_ref[...] = rows_ref[:, left_ref.shape[1] :].astype(BF16)


def copied(pairs, sem):
    copies = [pltpu.make_async_copy(src, dst, sem.at[j]) for j, (src, dst) in enumerate(pairs)]
    for copy in copies:
        copy.start()
    for copy in copies:
        copy.wait()


def pack_kernel(at_ref, gate_ref, up_ref, down_ref, out_ref, sem):
    units, part = gate_ref.shape[0], out_ref.shape[1]
    columns = pl.ds(pl.multiple_of(at_ref[0] * part, part), part)
    copied(
        [
            (ref.at[:, columns], out_ref.at[pl.ds(j * units, units), :])
            for j, ref in enumerate((gate_ref, up_ref, down_ref))
        ],
        sem,
    )


def weights_kernel(at_ref, gate_ref, up_ref, down_ref, got_ref, in_ref, out_ref, sem):
    units, part = gate_ref.shape[0], in_ref.shape[1]
    columns = pl.ds(pl.multiple_of(at_ref[0] * part, part), part)
    copied(
        [
            (gate_ref.at[:, columns], in_ref.at[pl.ds(0, units), :]),
            (up_ref.at[:, columns], in_ref.at[pl.ds(units, units), :]),
            (got_ref.at[pl.ds(0, 2 * units), :], in_ref.at[pl.ds(2 * units, 2 * units), :]),
            (down_ref.at[:, columns], out_ref.at[pl.ds(0, units), :]),
            (got_ref.at[pl.ds(2 * units, units), :], out_ref.at[pl.ds(units, units), :]),
        ],
        sem,
    )


def moved(kernel, out_shape, count, *args, at=None, params=PARAMS):
    return pl.pallas_call(
        kernel,
        out_shape=out_shape,
        in_specs=([] if at is None else [SMEM]) + [ANY] * len(args),
        out_specs=jax.tree.map(lambda _: ANY, out_shape),
        scratch_shapes=[pltpu.SemaphoreType.DMA((count,))],
        compiler_params=params,
    )(*([] if at is None else [at]), *args)


def stack_kernel(*refs, place):
    *block_refs, left_ref, right_ref, out_ref, sem = refs
    height, middle = left_ref.shape
    width = out_ref.shape[1]
    places = [k for k in range(len(block_refs) + 1) if k != place]
    at = pl.ds(place * height, height)
    copied(
        [
            *(
                (ref, out_ref.at[pl.ds(k * height, height), :])
                for k, ref in zip(places, block_refs, strict=True)
            ),
            (left_ref, out_ref.at[at, pl.ds(0, middle)]),
            (right_ref, out_ref.at[at, pl.ds(middle, width - middle)]),
        ],
        sem,
    )


def middle_kernel(sum_ref, got_ref, hid_ref, hid_got_ref, out_ref):
    units = hid_ref.shape[0]
    gate_value = sum_ref[:units, :] + got_ref[:units, :]
    up_value = sum_ref[units:, :] + got_ref[units:, :]
    hidden_grad = hid_ref[...] + hid_got_ref[...]
    gate_sigmoid = jax.nn.sigmoid(gate_value)
    swish_gate = gate_value * gate_sigmoid
    gate_grad = hidden_grad * up_value * gate_sigmoid * (1.0 + gate_value * (1.0 - gate_sigmoid))
    out_ref[:units, :] = gate_grad.astype(BF16)
    out_ref[units : 2 * units, :] = (hidden_grad * swish_gate).astype(BF16)
    out_ref[2 * units :, :] = (swish_gate * up_value).astype(BF16)


def pair_kernel(own_ref, got_ref, in_ref, hidden_ref):
    double = in_ref.shape[0] // 2
    in_ref[:double, :] = own_ref[:double, :]
    in_ref[double:, :] = got_ref[:double, :]
    hidden_ref[: double // 2, :] = own_ref[double:, :]
    hidden_ref[double // 2 :, :] = got_ref[double:, :]


def turn_kernel(_, left_ref, right_ref, came_ref, out_ref, *, whole, up):
    width = left_ref.shape[1]
    left, right = left_ref[...], right_ref[...]
    if whole or up:
        left = left + came_ref[:, :width].astype(F32)
    if whole or not up:
        right = right + came_ref[:, came_ref.shape[1] - width :].astype(F32)
    out_ref[:, :width] = left.astype(BF16)
    out_ref[:, width:] = right.astype(BF16)


def close_kernel(_, left_ref, right_ref, came_up_ref, came_down_ref, out_ref, rows_ref):
    n, pair, _ = out_ref.shape
    width = left_ref.shape[1]
    came = came_up_ref[...].astype(F32) + came_down_ref[...].astype(F32)
    rows_ref[:, :width] = left_ref[...] + came[:, :width]
    rows_ref[:, width:] = right_ref[...] + came[:, width:]
    for j in range(n):
        out_ref[j] = rows_ref[j * pair : (j + 1) * pair, :].astype(BF16)


def total_kernel(blocks_ref, mixed_ref, input_ref, *, quarters):
    part = mixed_ref.shape[1] // quarters
    for q in range(quarters):
        total = blocks_ref[q].astype(F32)
        for j in range(1, blocks_ref.shape[0] // quarters):
            total = total + blocks_ref[j * quarters + q].astype(F32)
        total = total.astype(BF16)
        mixed_ref[:, q * part : (q + 1) * part] = total[:, :part]
        input_ref[:, q * part : (q + 1) * part] = total[:, part:]


def rings_gathered(first, second):
    count = lax.axis_size("z")
    half, middle = count // 2, first.shape[1] // 2
    lead, kept, late = [first] * (count + 1), [first] * (count + 1), [second] * (count + 1)

    def step(ring, k):
        if k < half:
            return shifted(ring[k - 1], "z", -1), shifted(ring[1 - k], "z", 1)
        return (
            shifted(ring[k - 1][:, :middle], "z", -1),
            shifted(ring[1 - k][:, middle:], "z", 1),
        )

    for k in range(1, half + 1):
        lead[k], lead[-k] = step(lead, k)
        kept[k], kept[-k], late[k - 1], late[1 - k] = lax.optimization_barrier(
            (lead[k], lead[-k], late[k - 1], late[1 - k])
        )
        late[k], late[-k] = step(late, k)
    return kept, late


def stacked(ring):
    half = (len(ring) - 1) // 2
    height, width = ring[0].shape
    blocks = [*ring[:half], *ring[-half + 1 :][: half - 1]]
    return moved(
        functools.partial(stack_kernel, place=half),
        shape_of((2 * half * height, width)),
        2 * half + 1,
        *blocks,
        ring[half],
        ring[-half],
    )


def rings_reduced(factors, height, pair):
    count = lax.axis_size("z")
    half = count // 2
    width = factors[0][1].shape[1]
    lefts = [left for left, _ in factors]
    terms = {}

    def multiply(first, last):
        found = [
            by_columns(left[:, first * height : last * height], right)
            for left, (_, right) in zip(lefts, factors, strict=True)
        ]
        for k in range(first, last):
            terms[k] = found, k - first

    def added(kernel, out_shape, k, *came, scratch=(), **kwargs):
        found, j = terms[k % count]
        place = ((height, width), lambda *_: (j, 0))
        places = [place, place] + [None] * len(came)
        return called_at(kernel, out_shape, places, *found, *came, scratch=scratch, **kwargs)

    multiply(half - 2, half + 2)
    found, j = terms[half]
    up, down = (f[j * height : (j + 1) * height].astype(BF16) for f in found)
    both = shape_of((height, 2 * width))
    for k in range(half - 1, 0, -1):
        up, down = shifted(up, "z", 1), shifted(down, "z", -1)
        if k == half - 1:
            up, down, *lefts = lax.optimization_barrier((up, down, *lefts))
            multiply(half + 2, count)
            multiply(0, half - 2)
        up = added(turn_kernel, both, k, up, whole=k < half - 1, up=True)
        down = added(turn_kernel, both, -k, down, whole=k < half - 1, up=False)
    up, down = shifted(up, "z", 1), shifted(down, "z", -1)
    summed = added(
        close_kernel,
        shape_of((height // pair, pair, 2 * width)),
        0,
        up,
        down,
        scratch=[pltpu.VMEM((height, 2 * width), F32)],
    )
    return summed, lefts


def local(tokens, upstream, gate_weight, up_weight, down_weight):
    core = lax.axis_index("core")
    tok = lax.axis_index("tok")
    n_z = lax.axis_size("z")
    n_plane = lax.axis_size("y") * lax.axis_size("x")
    n_core = lax.axis_size("core")
    quarters = n_core * lax.axis_size("tok")
    pair, width = tokens.shape
    part = width // quarters
    units = gate_weight.shape[0]
    n = pair * quarters
    n_rows = n_plane * n
    count = n_z * n_plane * n
    own_at = (tok * n_core + core).astype(jnp.int32).reshape(1)
    other_at = (tok * n_core + 1 - core).astype(jnp.int32).reshape(1)

    dealt = called(
        deal_kernel,
        shape_of((n_plane * quarters, pair, 2 * part)),
        tokens,
        upstream,
        quarters=quarters,
    )
    dealt, *weights = lax.optimization_barrier((dealt, gate_weight, up_weight, down_weight))
    sent = moved(pack_kernel, shape_of((3 * units, part)), 3, *weights, at=other_at, params=LARGE)
    in_weights, out_weights = moved(
        weights_kernel,
        (shape_of((4 * units, part)), shape_of((2 * units, part))),
        5,
        *weights,
        shifted(sent, "core", 1),
        at=own_at,
        params=LARGE,
    )
    dealt = exchanged(dealt, (*PLANE, *PAIRS))
    dealt, in_weights, out_weights = lax.optimization_barrier((dealt, in_weights, out_weights))
    rows, grads = called(
        merge_kernel,
        (shape_of((n_rows, part)), shape_of((n_rows, part))),
        dealt,
        scratch=[pltpu.VMEM((n_rows, 2 * part), F32)],
    )
    rows, grads = rings_gathered(rows, grads)
    rows = stacked(rows)

    gate_up = shifted(by_rows(in_weights[2 * units :], rows), "core", 1)
    gate_up = by_rows(in_weights[: 2 * units], rows) + gate_up
    grads = stacked(grads)
    hidden_grad = shifted(by_rows(out_weights[units:], grads), "core", 1)
    hidden_grad = by_rows(out_weights[:units], grads) + hidden_grad
    own = called(
        middle_kernel,
        shape_of((3 * units, count)),
        gate_up,
        shifted(gate_up, "tok", 1),
        hidden_grad,
        shifted(hidden_grad, "tok", 1),
    )
    in_grads, hidden = called(
        pair_kernel,
        (shape_of((4 * units, count)), shape_of((2 * units, count))),
        own,
        shifted(own, "core", 1),
    )

    summed, (hidden, in_grads) = rings_reduced(
        [(hidden, out_weights), (in_grads, in_weights)], n_rows, pair
    )
    mixed, input_grad = called(
        total_kernel,
        (shape_of((pair, width)), shape_of((pair, width))),
        exchanged(summed, (*PLANE, *PAIRS)),
        quarters=quarters,
    )

    def product(left, right):
        return jnp.dot(left, right, preferred_element_type=F32).astype(BF16)

    got_in = shifted(product(in_grads[2 * units :], rows), "core", 1)
    got_out = shifted(product(hidden[units:], grads), "core", 1)
    in_weight_grad = product(in_grads[: 2 * units], rows)
    out_weight_grad = product(hidden[:units], grads)

    def side_by_side(mine, others):
        left = jnp.where(core == 0, mine, others)
        right = jnp.where(core == 0, others, mine)
        return jnp.concatenate([left, right], axis=1)

    return (
        mixed,
        input_grad,
        side_by_side(in_weight_grad[:units], got_in[:units]),
        side_by_side(in_weight_grad[units:], got_in[units:]),
        side_by_side(out_weight_grad, got_out),
    )


def solution(mesh):
    finer = Mesh(mesh.devices.reshape(8, 4, 2, 2, mesh.shape["tok"]), AXES)
    return jax.shard_map(
        local,
        mesh=finer,
        in_specs=(P(AXES, None), P(AXES, None), P(BLK, None), P(BLK, None), P(BLK, None)),
        out_specs=(P(AXES, None), P(AXES, None), P(BLK, "tok"), P(BLK, "tok"), P(BLK, "tok")),
        check_vma=False,
    )
```

```python
import functools

import jax
import jax.numpy as jnp
from jax import lax
from jax.experimental import pallas as pl
from jax.experimental.pallas import tpu as pltpu
from jax.sharding import Mesh
from jax.sharding import PartitionSpec as P

AXES = ("z", "y", "x", "core", "tok")
BLK = ("z", "y", "x", "core")
PLANE = ("y", "x")
PAIRS = ("tok", "core")
F32 = jnp.float32
BF16 = jnp.bfloat16
VMEM = pl.BlockSpec(memory_space=pltpu.VMEM)
SMEM = pl.BlockSpec(memory_space=pltpu.SMEM)
PARAMS = pltpu.CompilerParams(vmem_limit_bytes=20 * 1024 * 1024)
LARGE = pltpu.CompilerParams(vmem_limit_bytes=58 * 1024 * 1024)


def shifted(block, axis, distance):
    count = lax.axis_size(axis)
    return lax.ppermute(block, axis, [(i, (i + distance) % count) for i in range(count)])


def exchanged(blocks, axes):
    return lax.all_to_all(blocks, axes, 0, 0, tiled=True)


def by_rows(left, right):
    return lax.dot_general(left, right, (((1,), (1,)), ((), ())), preferred_element_type=F32)


def by_columns(left, right):
    return lax.dot_general(left, right, (((0,), (0,)), ((), ())), preferred_element_type=F32)


def called(kernel, out_shape, *args, specs=None, scratch=(), **kwargs):
    specs = specs or [VMEM] * len(args)
    return pl.pallas_call(
        functools.partial(kernel, **kwargs),
        out_shape=out_shape,
        in_specs=specs,
        out_specs=jax.tree.map(lambda _: VMEM, out_shape),
        scratch_shapes=scratch,
        compiler_params=PARAMS,
    )(*args)


def called_at(kernel, out_shape, places, *args, index=None, scratch=(), params=PARAMS, **kwargs):
    def whole(shape):
        return pl.BlockSpec(shape, lambda *_: (0,) * len(shape))

    specs = [
        whole(arg.shape) if place is None else pl.BlockSpec(*place)
        for arg, place in zip(args, places, strict=True)
    ]
    grid = pltpu.PrefetchScalarGridSpec(
        num_scalar_prefetch=1,
        grid=(1,),
        in_specs=specs,
        out_specs=jax.tree.map(lambda o: whole(o.shape), out_shape),
        scratch_shapes=scratch,
    )
    return pl.pallas_call(
        functools.partial(kernel, **kwargs),
        out_shape=out_shape,
        grid_spec=grid,
        compiler_params=params,
    )(jnp.zeros((1,), jnp.int32) if index is None else index, *args)


def shape_of(shape, kind=BF16):
    return jax.ShapeDtypeStruct(shape, kind)


def deal_kernel(tokens_ref, upstream_ref, out_ref, *, quarters):
    part = tokens_ref.shape[1] // quarters
    for q in range(quarters):
        rows = tokens_ref[:, q * part : (q + 1) * part]
        grads = upstream_ref[:, q * part : (q + 1) * part]
        for j in range(out_ref.shape[0] // quarters):
            out_ref[j * quarters + q, :, :part] = rows
            out_ref[j * quarters + q, :, part:] = grads


def merge_kernel(blocks_ref, out_ref, rows_ref):
    n, pair, _ = blocks_ref.shape
    for j in range(n):
        rows_ref[j * pair : (j + 1) * pair, :] = blocks_ref[j].astype(F32)
    out_ref[...] = rows_ref[...].astype(BF16)


def pack_kernel(_, gate_ref, up_ref, down_ref, out_ref):
    units = gate_ref.shape[0]
    for j, ref in enumerate((gate_ref, up_ref, down_ref)):
        out_ref[j * units : (j + 1) * units, :] = ref[...]


def weights_kernel(_, gate_ref, up_ref, down_ref, got_ref, in_ref, out_ref):
    units = gate_ref.shape[0]
    in_ref[:units, :] = gate_ref[...]
    in_ref[units : 2 * units, :] = up_ref[...]
    in_ref[2 * units :, :] = got_ref[: 2 * units, :]
    out_ref[:units, :] = down_ref[...]
    out_ref[units:, :] = got_ref[2 * units :, :]


def stack_kernel(*refs):
    *block_refs, rows_ref, grads_ref = refs
    part = rows_ref.shape[1]
    k = 0
    for ref in block_refs:
        height, width = ref.shape
        at = slice(k * height, (k + 1) * height)
        if width == 2 * part:
            rows_ref[at, :] = ref[:, :part]
            grads_ref[at, :] = ref[:, part:]
            k += 1
        elif ref is block_refs[-2]:
            rows_ref[at, :] = ref[...]
        else:
            grads_ref[at, :] = ref[...]
            k += 1


def partial_kernel(rows_ref, grads_ref, in_ref, out_ref, own_ref, other_ref):
    units = out_ref.shape[0] // 2
    rows, grads = rows_ref[...], grads_ref[...]
    for j, ref in enumerate((own_ref, other_ref)):
        ref[: 2 * units, :] = by_rows(in_ref[2 * j * units : 2 * (j + 1) * units, :], rows)
        ref[2 * units :, :] = by_rows(out_ref[j * units : (j + 1) * units, :], grads)


def middle_kernel(sum_ref, got_ref, out_ref):
    units = sum_ref.shape[0] // 3
    total = sum_ref[...] + got_ref[...]
    gate_value, up_value = total[:units, :], total[units : 2 * units, :]
    hidden_grad = total[2 * units :, :]
    gate_sigmoid = jax.nn.sigmoid(gate_value)
    swish_gate = gate_value * gate_sigmoid
    gate_grad = hidden_grad * up_value * gate_sigmoid * (1.0 + gate_value * (1.0 - gate_sigmoid))
    out_ref[:units, :] = gate_grad.astype(BF16)
    out_ref[units : 2 * units, :] = (hidden_grad * swish_gate).astype(BF16)
    out_ref[2 * units :, :] = (swish_gate * up_value).astype(BF16)


def pair_kernel(own_ref, got_ref, in_ref, hidden_ref):
    double = in_ref.shape[0] // 2
    in_ref[:double, :] = own_ref[:double, :]
    in_ref[double:, :] = got_ref[:double, :]
    hidden_ref[: double // 2, :] = own_ref[double:, :]
    hidden_ref[double // 2 :, :] = got_ref[double:, :]


def turn_kernel(_, left_ref, right_ref, came_ref, out_ref, *, whole, up):
    width = left_ref.shape[1]
    left, right = left_ref[...], right_ref[...]
    if whole or up:
        left = left + came_ref[:, :width].astype(F32)
    if whole or not up:
        right = right + came_ref[:, came_ref.shape[1] - width :].astype(F32)
    out_ref[:, :width] = left.astype(BF16)
    out_ref[:, width:] = right.astype(BF16)


def close_kernel(_, left_ref, right_ref, came_up_ref, came_down_ref, out_ref, rows_ref):
    n, pair, _ = out_ref.shape
    width = left_ref.shape[1]
    came = came_up_ref[...].astype(F32) + came_down_ref[...].astype(F32)
    rows_ref[:, :width] = left_ref[...] + came[:, :width]
    rows_ref[:, width:] = right_ref[...] + came[:, width:]
    for j in range(n):
        out_ref[j] = rows_ref[j * pair : (j + 1) * pair, :].astype(BF16)


def total_kernel(blocks_ref, mixed_ref, input_ref, *, quarters):
    part = mixed_ref.shape[1] // quarters
    for q in range(quarters):
        total = blocks_ref[q].astype(F32)
        for j in range(1, blocks_ref.shape[0] // quarters):
            total = total + blocks_ref[j * quarters + q].astype(F32)
        total = total.astype(BF16)
        mixed_ref[:, q * part : (q + 1) * part] = total[:, :part]
        input_ref[:, q * part : (q + 1) * part] = total[:, part:]


def ring_reduced(terms, later, height, pair):
    count = lax.axis_size("z")
    half = count // 2

    def added(kernel, out_shape, k, *came, scratch=(), **kwargs):
        found, j = terms[k % count]
        place = ((height, found[0].shape[1]), lambda *_: (j, 0))
        places = [place, place] + [None] * len(came)
        return called_at(kernel, out_shape, places, *found, *came, scratch=scratch, **kwargs)

    found, j = terms[half]
    width = found[0].shape[1]
    up, down = (f[j * height : (j + 1) * height].astype(BF16) for f in found)
    both = shape_of((height, 2 * width))
    for k in range(half - 1, 0, -1):
        up, down = shifted(up, "z", 1), shifted(down, "z", -1)
        if k in later:
            up, down = later[k](up, down)
        up = added(turn_kernel, both, k, up, whole=k < half - 1, up=True)
        down = added(turn_kernel, both, -k, down, whole=k < half - 1, up=False)
    up, down = shifted(up, "z", 1), shifted(down, "z", -1)
    return added(
        close_kernel,
        shape_of((height // pair, pair, 2 * width)),
        0,
        up,
        down,
        scratch=[pltpu.VMEM((height, 2 * width), F32)],
    )


def local(tokens, upstream, gate_weight, up_weight, down_weight):
    core = lax.axis_index("core")
    tok = lax.axis_index("tok")
    n_z = lax.axis_size("z")
    n_plane = lax.axis_size("y") * lax.axis_size("x")
    n_core = lax.axis_size("core")
    quarters = n_core * lax.axis_size("tok")
    pair, width = tokens.shape
    part = width // quarters
    units = gate_weight.shape[0]
    n = pair * quarters
    n_rows = n_plane * n
    own_at = (tok * n_core + core).astype(jnp.int32).reshape(1)
    other_at = (tok * n_core + 1 - core).astype(jnp.int32).reshape(1)

    dealt = called(
        deal_kernel,
        shape_of((n_plane * quarters, pair, 2 * part)),
        tokens,
        upstream,
        quarters=quarters,
    )
    dealt, *weights = lax.optimization_barrier((dealt, gate_weight, up_weight, down_weight))
    column = ((units, part), lambda i, at: (0, at[0]))
    sent = called_at(
        pack_kernel,
        shape_of((3 * units, part)),
        [column] * 3,
        *weights,
        index=other_at,
        params=LARGE,
    )
    in_weights, out_weights = called_at(
        weights_kernel,
        (shape_of((4 * units, part)), shape_of((2 * units, part))),
        [column] * 3 + [None],
        *weights,
        shifted(sent, "core", 1),
        index=own_at,
        params=LARGE,
    )
    dealt = exchanged(dealt, (*PLANE, *PAIRS))
    dealt, in_weights, out_weights = lax.optimization_barrier((dealt, in_weights, out_weights))
    block = called(
        merge_kernel,
        shape_of((n_rows, 2 * part)),
        dealt,
        scratch=[pltpu.VMEM((n_rows, 2 * part), F32)],
    )

    def stacked(*blocks):
        shape = shape_of((half * n_rows, part))
        return called(stack_kernel, (shape, shape), *blocks)

    def partial_sums(rows, grads):
        shape = shape_of((3 * units, rows.shape[0]), F32)
        return called(partial_kernel, (shape, shape), rows, grads, in_weights, out_weights)

    def factors(sums, got):
        own = called(middle_kernel, shape_of(sums.shape), sums, got)
        return called(
            pair_kernel,
            (
                shape_of((4 * units, sums.shape[1])),
                shape_of((2 * units, sums.shape[1])),
            ),
            own,
            shifted(own, "core", 1),
        )

    half = n_z // 2
    ring = {0: block}
    for k in range(1, half):
        ring[k], ring[-k] = shifted(ring[k - 1], "z", -1), shifted(ring[1 - k], "z", 1)
    near_rows, near_grads = stacked(*(ring[k] for k in range(-half // 2, half // 2)))
    own, other = partial_sums(near_rows, near_grads)
    ahead, behind, own, other = lax.optimization_barrier((ring[half - 1], ring[1 - half], own, other))
    left, right = shifted(ahead[:, :part], "z", -1), shifted(behind[:, part:], "z", 1)
    left, right, near_sums = lax.optimization_barrier(
        (left, right, own + shifted(other, "core", 1))
    )
    near_got = shifted(near_sums, "tok", 1)
    far_rows, far_grads = stacked(
        *(ring[k] for k in range(half // 2, half)),
        *(ring[k] for k in range(1 - half, -half // 2)),
        left,
        right,
    )
    own, other = partial_sums(far_rows, far_grads)
    far_sums = own + shifted(other, "core", 1)
    far_in, far_hidden = factors(far_sums, shifted(far_sums, "tok", 1))
    near_in, near_hidden = factors(near_sums, near_got)

    terms = {}

    def set_terms(places, hidden, in_grads):
        found = (by_columns(hidden, out_weights), by_columns(in_grads, in_weights))
        for j, k in enumerate(places):
            terms[k % n_z] = found, j

    far_places = [*range(half // 2, half), *range(1 - half, -half // 2), half]
    set_terms(far_places, far_hidden, far_in)
    grads_out = []

    def near_terms(up, down):
        nonlocal near_in, near_hidden
        up, down, near_in, near_hidden = lax.optimization_barrier(
            (up, down, near_in, near_hidden)
        )
        set_terms(range(-half // 2, half // 2), near_hidden, near_in)
        return up, down

    def weight_product(near, far, near_right, far_right):
        total = jnp.dot(near, near_right, preferred_element_type=F32)
        total = total + jnp.dot(far, far_right, preferred_element_type=F32)
        return total.astype(BF16)

    def others_grads(up, down):
        up, down, a, b, c, d = lax.optimization_barrier(
            (up, down, near_in, far_in, near_hidden, far_hidden)
        )
        in_other = weight_product(a[2 * units :], b[2 * units :], near_rows, far_rows)
        out_other = weight_product(c[units:], d[units:], near_grads, far_grads)
        grads_out.extend([shifted(in_other, "core", 1), shifted(out_other, "core", 1)])
        return up, down

    def own_grads(up, down):
        up, down, a, b, c, d = lax.optimization_barrier(
            (up, down, near_in, far_in, near_hidden, far_hidden)
        )
        grads_out.append(weight_product(a[: 2 * units], b[: 2 * units], near_rows, far_rows))
        grads_out.append(weight_product(c[:units], d[:units], near_grads, far_grads))
        return up, down

    later = {half - 1: near_terms, half - 2: others_grads, half - 3: own_grads}
    summed = ring_reduced(terms, later, n_rows, pair)
    mixed, input_grad = called(
        total_kernel,
        (shape_of((pair, width)), shape_of((pair, width))),
        exchanged(summed, (*PLANE, *PAIRS)),
        quarters=quarters,
    )
    got_in, got_out, in_weight_grad, out_weight_grad = grads_out

    def side_by_side(mine, others):
        left = jnp.where(core == 0, mine, others)
        right = jnp.where(core == 0, others, mine)
        return jnp.concatenate([left, right], axis=1)

    return (
        mixed,
        input_grad,
        side_by_side(in_weight_grad[:units], got_in[:units]),
        side_by_side(in_weight_grad[units:], got_in[units:]),
        side_by_side(out_weight_grad, got_out),
    )


def solution(mesh):
    finer = Mesh(mesh.devices.reshape(8, 4, 2, 2, mesh.shape["tok"]), AXES)
    return jax.shard_map(
        local,
        mesh=finer,
        in_specs=(P(AXES, None), P(AXES, None), P(BLK, None), P(BLK, None), P(BLK, None)),
        out_specs=(P(AXES, None), P(AXES, None), P(BLK, "tok"), P(BLK, "tok"), P(BLK, "tok")),
        check_vma=False,
    )
```

```python
import functools

import jax
import jax.numpy as jnp
from jax import lax
from jax.experimental import pallas as pl
from jax.experimental.pallas import tpu as pltpu
from jax.sharding import Mesh
from jax.sharding import PartitionSpec as P

AXES = ("z", "y", "x", "core", "tok")
BLK = ("z", "y", "x", "core")
PLANE = ("y", "x")
PAIRS = ("tok", "core")
F32 = jnp.float32
BF16 = jnp.bfloat16
VMEM = pl.BlockSpec(memory_space=pltpu.VMEM)
SMEM = pl.BlockSpec(memory_space=pltpu.SMEM)
PARAMS = pltpu.CompilerParams(vmem_limit_bytes=20 * 1024 * 1024)
LARGE = pltpu.CompilerParams(vmem_limit_bytes=58 * 1024 * 1024)


def shifted(block, axis, distance):
    count = lax.axis_size(axis)
    return lax.ppermute(block, axis, [(i, (i + distance) % count) for i in range(count)])


def exchanged(blocks, axes):
    return lax.all_to_all(blocks, axes, 0, 0, tiled=True)


def by_rows(left, right):
    return lax.dot_general(left, right, (((1,), (1,)), ((), ())), preferred_element_type=F32)


def by_columns(left, right):
    return lax.dot_general(left, right, (((0,), (0,)), ((), ())), preferred_element_type=F32)


def called(kernel, out_shape, *args, specs=None, scratch=(), **kwargs):
    specs = specs or [VMEM] * len(args)
    return pl.pallas_call(
        functools.partial(kernel, **kwargs),
        out_shape=out_shape,
        in_specs=specs,
        out_specs=jax.tree.map(lambda _: VMEM, out_shape),
        scratch_shapes=scratch,
        compiler_params=PARAMS,
    )(*args)


def called_at(kernel, out_shape, places, *args, index=None, scratch=(), params=PARAMS, **kwargs):
    def whole(shape):
        return pl.BlockSpec(shape, lambda *_: (0,) * len(shape))

    specs = [
        whole(arg.shape) if place is None else pl.BlockSpec(*place)
        for arg, place in zip(args, places, strict=True)
    ]
    grid = pltpu.PrefetchScalarGridSpec(
        num_scalar_prefetch=1,
        grid=(1,),
        in_specs=specs,
        out_specs=jax.tree.map(lambda o: whole(o.shape), out_shape),
        scratch_shapes=scratch,
    )
    return pl.pallas_call(
        functools.partial(kernel, **kwargs),
        out_shape=out_shape,
        grid_spec=grid,
        compiler_params=params,
    )(jnp.zeros((1,), jnp.int32) if index is None else index, *args)


def shape_of(shape, kind=BF16):
    return jax.ShapeDtypeStruct(shape, kind)


def deal_kernel(tokens_ref, upstream_ref, out_ref, *, quarters):
    part = tokens_ref.shape[1] // quarters
    for q in range(quarters):
        rows = tokens_ref[:, q * part : (q + 1) * part]
        grads = upstream_ref[:, q * part : (q + 1) * part]
        for j in range(out_ref.shape[0] // quarters):
            out_ref[j * quarters + q, :, :part] = rows
            out_ref[j * quarters + q, :, part:] = grads


def merge_kernel(blocks_ref, left_ref, right_ref, rows_ref):
    n, pair, _ = blocks_ref.shape
    for j in range(n):
        rows_ref[j * pair : (j + 1) * pair, :] = blocks_ref[j].astype(F32)
    left_ref[...] = rows_ref[:, : left_ref.shape[1]].astype(BF16)
    right_ref[...] = rows_ref[:, left_ref.shape[1] :].astype(BF16)


def pack_kernel(_, gate_ref, up_ref, down_ref, out_ref):
    units = gate_ref.shape[0]
    for j, ref in enumerate((gate_ref, up_ref, down_ref)):
        out_ref[j * units : (j + 1) * units, :] = ref[...]


def weights_kernel(_, gate_ref, up_ref, down_ref, got_ref, in_ref, out_ref):
    units = gate_ref.shape[0]
    in_ref[:units, :] = gate_ref[...]
    in_ref[units : 2 * units, :] = up_ref[...]
    in_ref[2 * units :, :] = got_ref[: 2 * units, :]
    out_ref[:units, :] = down_ref[...]
    out_ref[units:, :] = got_ref[2 * units :, :]


def stack_kernel(*refs):
    *block_refs, out_ref = refs
    width = out_ref.shape[1]
    row, column = 0, 0
    for ref in block_refs:
        height, columns = ref.shape
        out_ref[row : row + height, column : column + columns] = ref[...]
        column += columns
        if column == width:
            row, column = row + height, 0


def partial_kernel(rows_ref, grads_ref, in_ref, out_ref, own_ref, other_ref):
    units = out_ref.shape[0] // 2
    rows, grads = rows_ref[...], grads_ref[...]
    for j, ref in enumerate((own_ref, other_ref)):
        ref[: 2 * units, :] = by_rows(in_ref[2 * j * units : 2 * (j + 1) * units, :], rows)
        ref[2 * units :, :] = by_rows(out_ref[j * units : (j + 1) * units, :], grads)


def middle_kernel(sum_ref, got_ref, out_ref):
    units = sum_ref.shape[0] // 3
    total = sum_ref[...] + got_ref[...]
    gate_value, up_value = total[:units, :], total[units : 2 * units, :]
    hidden_grad = total[2 * units :, :]
    gate_sigmoid = jax.nn.sigmoid(gate_value)
    swish_gate = gate_value * gate_sigmoid
    gate_grad = hidden_grad * up_value * gate_sigmoid * (1.0 + gate_value * (1.0 - gate_sigmoid))
    out_ref[:units, :] = gate_grad.astype(BF16)
    out_ref[units : 2 * units, :] = (hidden_grad * swish_gate).astype(BF16)
    out_ref[2 * units :, :] = (swish_gate * up_value).astype(BF16)


def pair_kernel(own_ref, got_ref, in_ref, hidden_ref):
    double = in_ref.shape[0] // 2
    in_ref[:double, :] = own_ref[:double, :]
    in_ref[double:, :] = got_ref[:double, :]
    hidden_ref[: double // 2, :] = own_ref[double:, :]
    hidden_ref[double // 2 :, :] = got_ref[double:, :]


def turn_kernel(_, term_ref, came_ref, out_ref, *, up):
    width, reach = term_ref.shape[1], came_ref.shape[1]
    start = 0 if up else width - reach
    if reach < width:
        out_ref[...] = term_ref[...].astype(BF16)
    total = term_ref[:, start : start + reach] + came_ref[...].astype(F32)
    out_ref[:, start : start + reach] = total.astype(BF16)


def close_kernel(_, a0_ref, b0_ref, a1_ref, a2_ref, b1_ref, b2_ref, out_ref, rows_ref):
    n, pair, _ = out_ref.shape
    width = a0_ref.shape[1]
    rows_ref[:, :width] = a0_ref[...] + a1_ref[...].astype(F32) + a2_ref[...].astype(F32)
    rows_ref[:, width:] = b0_ref[...] + b1_ref[...].astype(F32) + b2_ref[...].astype(F32)
    for j in range(n):
        out_ref[j] = rows_ref[j * pair : (j + 1) * pair, :].astype(BF16)


def total_kernel(blocks_ref, mixed_ref, input_ref, *, quarters):
    part = mixed_ref.shape[1] // quarters
    for q in range(quarters):
        total = blocks_ref[q].astype(F32)
        for j in range(1, blocks_ref.shape[0] // quarters):
            total = total + blocks_ref[j * quarters + q].astype(F32)
        total = total.astype(BF16)
        mixed_ref[:, q * part : (q + 1) * part] = total[:, :part]
        input_ref[:, q * part : (q + 1) * part] = total[:, part:]


def ring_reduced(terms, later, height, pair):
    count = lax.axis_size("z")
    half = count // 2

    def at(k):
        found, j = terms[k % count]
        place = ((height, found[0].shape[1]), lambda *_: (j, 0))
        return found, place

    def turned(ring, k, came, up):
        found, place = at(k)
        term = found[ring]
        out = shape_of((height, term.shape[1]))
        return called_at(turn_kernel, out, [place, None], term, came, up=up)

    found, j = terms[half]
    width = found[0].shape[1]
    rings = []
    for f in found:
        term = f[j * height : (j + 1) * height].astype(BF16)
        rings.append([term[:, : width // 2], term[:, width // 2 :]])
    for k in range(half - 1, 0, -1):
        for j, (up, down) in enumerate(rings):
            rings[j] = [shifted(up, "z", 1), shifted(down, "z", -1)]
        if k in later:
            rings[0][0], rings[0][1] = later[k](*rings[0])
        for j, (up, down) in enumerate(rings):
            rings[j] = [turned(j, k, up, True), turned(j, -k, down, False)]
    came = [c for up, down in rings for c in (shifted(up, "z", 1), shifted(down, "z", -1))]
    found, place = at(0)
    return called_at(
        close_kernel,
        shape_of((height // pair, pair, 2 * width)),
        [place, place] + [None] * len(came),
        *found,
        *came,
        scratch=[pltpu.VMEM((height, 2 * width), F32)],
    )


def local(tokens, upstream, gate_weight, up_weight, down_weight):
    core = lax.axis_index("core")
    tok = lax.axis_index("tok")
    n_z = lax.axis_size("z")
    n_plane = lax.axis_size("y") * lax.axis_size("x")
    n_core = lax.axis_size("core")
    quarters = n_core * lax.axis_size("tok")
    pair, width = tokens.shape
    part = width // quarters
    units = gate_weight.shape[0]
    n = pair * quarters
    n_rows = n_plane * n
    own_at = (tok * n_core + core).astype(jnp.int32).reshape(1)
    other_at = (tok * n_core + 1 - core).astype(jnp.int32).reshape(1)

    dealt = called(
        deal_kernel,
        shape_of((n_plane * quarters, pair, 2 * part)),
        tokens,
        upstream,
        quarters=quarters,
    )
    dealt, *weights = lax.optimization_barrier((dealt, gate_weight, up_weight, down_weight))
    column = ((units, part), lambda i, at: (0, at[0]))
    sent = called_at(
        pack_kernel,
        shape_of((3 * units, part)),
        [column] * 3,
        *weights,
        index=other_at,
        params=LARGE,
    )
    in_weights, out_weights = called_at(
        weights_kernel,
        (shape_of((4 * units, part)), shape_of((2 * units, part))),
        [column] * 3 + [None],
        *weights,
        shifted(sent, "core", 1),
        index=own_at,
        params=LARGE,
    )
    dealt = exchanged(dealt, (*PLANE, *PAIRS))
    dealt, in_weights, out_weights = lax.optimization_barrier((dealt, in_weights, out_weights))
    blocks = called(
        merge_kernel,
        (shape_of((n_rows, part)), shape_of((n_rows, part))),
        dealt,
        scratch=[pltpu.VMEM((n_rows, 2 * part), F32)],
    )

    def stacked(*blocks):
        return called(stack_kernel, shape_of((half * n_rows, part)), *blocks)

    def partial_sums(rows, grads):
        shape = shape_of((3 * units, rows.shape[0]), F32)
        return called(partial_kernel, (shape, shape), rows, grads, in_weights, out_weights)

    def factors(sums, got):
        own = called(middle_kernel, shape_of(sums.shape), sums, got)
        return called(
            pair_kernel,
            (
                shape_of((4 * units, sums.shape[1])),
                shape_of((2 * units, sums.shape[1])),
            ),
            own,
            shifted(own, "core", 1),
        )

    half = n_z // 2
    rings = [{0: block} for block in blocks]
    for k in range(1, half):
        for ring in rings:
            ring[k], ring[-k] = shifted(ring[k - 1], "z", -1), shifted(ring[1 - k], "z", 1)
    near_rows, near_grads = (
        stacked(*(ring[k] for k in range(-half // 2, half // 2))) for ring in rings
    )
    own, other = partial_sums(near_rows, near_grads)
    near_sums = own + shifted(other, "core", 1)
    edges = [[ring[half - 1], ring[1 - half]] for ring in rings]
    *edges[1], near_sums = lax.optimization_barrier((*edges[1], near_sums))
    ends = []
    for ahead, behind in edges:
        ends.append(shifted(ahead[:, : part // 2], "z", -1))
        ends.append(shifted(behind[:, part // 2 :], "z", 1))
    near_got = shifted(near_sums, "tok", 1)
    *ends, near_got = lax.optimization_barrier((*ends, near_got))
    far_rows, far_grads = (
        stacked(
            *(ring[k] for k in range(half // 2, half)),
            *(ring[k] for k in range(1 - half, -half // 2)),
            *end,
        )
        for ring, end in zip(rings, (ends[:2], ends[2:]), strict=True)
    )
    own, other = partial_sums(far_rows, far_grads)
    far_sums = own + shifted(other, "core", 1)
    far_got = shifted(far_sums, "tok", 1)
    near_in, near_hidden = factors(near_sums, near_got)
    far_got, near_in, near_hidden = lax.optimization_barrier((far_got, near_in, near_hidden))
    far_in, far_hidden = factors(far_sums, far_got)

    terms = {}

    def set_terms(places, hidden, in_grads):
        found = (by_columns(hidden, out_weights), by_columns(in_grads, in_weights))
        for j, k in enumerate(places):
            terms[k % n_z] = found, j

    far_places = [*range(half // 2, half), *range(1 - half, -half // 2), half]
    set_terms(far_places, far_hidden, far_in)
    grads_out = []

    def near_terms(up, down):
        nonlocal near_in, near_hidden
        up, down, near_in, near_hidden = lax.optimization_barrier(
            (up, down, near_in, near_hidden)
        )
        set_terms(range(-half // 2, half // 2), near_hidden, near_in)
        return up, down

    def weight_product(near, far, near_right, far_right):
        total = jnp.dot(near, near_right, preferred_element_type=F32)
        total = total + jnp.dot(far, far_right, preferred_element_type=F32)
        return total.astype(BF16)

    def others_grads(up, down):
        up, down, a, b, c, d = lax.optimization_barrier(
            (up, down, near_in, far_in, near_hidden, far_hidden)
        )
        in_other = weight_product(a[2 * units :], b[2 * units :], near_rows, far_rows)
        out_other = weight_product(c[units:], d[units:], near_grads, far_grads)
        grads_out.extend([shifted(in_other, "core", 1), shifted(out_other, "core", 1)])
        return up, down

    later = {half - 1: near_terms, half - 2: others_grads}
    summed, a, b, c, d = lax.optimization_barrier(
        (
            ring_reduced(terms, later, n_rows, pair),
            near_in,
            far_in,
            near_hidden,
            far_hidden,
        )
    )
    in_weight_grad = weight_product(a[: 2 * units], b[: 2 * units], near_rows, far_rows)
    out_weight_grad = weight_product(c[:units], d[:units], near_grads, far_grads)
    mixed, input_grad = called(
        total_kernel,
        (shape_of((pair, width)), shape_of((pair, width))),
        exchanged(summed, (*PLANE, *PAIRS)),
        quarters=quarters,
    )
    got_in, got_out = grads_out

    def side_by_side(mine, others):
        left = jnp.where(core == 0, mine, others)
        right = jnp.where(core == 0, others, mine)
        return jnp.concatenate([left, right], axis=1)

    return (
        mixed,
        input_grad,
        side_by_side(in_weight_grad[:units], got_in[:units]),
        side_by_side(in_weight_grad[units:], got_in[units:]),
        side_by_side(out_weight_grad, got_out),
    )


def solution(mesh):
    finer = Mesh(mesh.devices.reshape(8, 4, 2, 2, mesh.shape["tok"]), AXES)
    return jax.shard_map(
        local,
        mesh=finer,
        in_specs=(P(AXES, None), P(AXES, None), P(BLK, None), P(BLK, None), P(BLK, None)),
        out_specs=(P(AXES, None), P(AXES, None), P(BLK, "tok"), P(BLK, "tok"), P(BLK, "tok")),
        check_vma=False,
    )
```

```python
import functools

import jax
import jax.numpy as jnp
from jax import lax
from jax.experimental import pallas as pl
from jax.experimental.pallas import tpu as pltpu
from jax.sharding import Mesh
from jax.sharding import PartitionSpec as P

AXES = ("z", "y", "x", "core", "tok")
BLK = ("z", "y", "x", "core")
PLANE = ("y", "x")
PAIRS = ("tok", "core")
F32 = jnp.float32
BF16 = jnp.bfloat16
VMEM = pl.BlockSpec(memory_space=pltpu.VMEM)
SMEM = pl.BlockSpec(memory_space=pltpu.SMEM)
PARAMS = pltpu.CompilerParams(vmem_limit_bytes=20 * 1024 * 1024)
LARGE = pltpu.CompilerParams(vmem_limit_bytes=58 * 1024 * 1024)


def shifted(block, axis, distance):
    count = lax.axis_size(axis)
    return lax.ppermute(block, axis, [(i, (i + distance) % count) for i in range(count)])


def exchanged(blocks, axes):
    return lax.all_to_all(blocks, axes, 0, 0, tiled=True)


def by_rows(left, right):
    return lax.dot_general(left, right, (((1,), (1,)), ((), ())), preferred_element_type=F32)


def by_columns(left, right):
    return lax.dot_general(left, right, (((0,), (0,)), ((), ())), preferred_element_type=F32)


def called(kernel, out_shape, *args, specs=None, scratch=(), **kwargs):
    specs = specs or [VMEM] * len(args)
    return pl.pallas_call(
        functools.partial(kernel, **kwargs),
        out_shape=out_shape,
        in_specs=specs,
        out_specs=jax.tree.map(lambda _: VMEM, out_shape),
        scratch_shapes=scratch,
        compiler_params=PARAMS,
    )(*args)


def called_at(kernel, out_shape, places, *args, index=None, scratch=(), params=PARAMS, **kwargs):
    def whole(shape):
        return pl.BlockSpec(shape, lambda *_: (0,) * len(shape))

    specs = [
        whole(arg.shape) if place is None else pl.BlockSpec(*place)
        for arg, place in zip(args, places, strict=True)
    ]
    grid = pltpu.PrefetchScalarGridSpec(
        num_scalar_prefetch=1,
        grid=(1,),
        in_specs=specs,
        out_specs=jax.tree.map(lambda o: whole(o.shape), out_shape),
        scratch_shapes=scratch,
    )
    return pl.pallas_call(
        functools.partial(kernel, **kwargs),
        out_shape=out_shape,
        grid_spec=grid,
        compiler_params=params,
    )(jnp.zeros((1,), jnp.int32) if index is None else index, *args)


def shape_of(shape, kind=BF16):
    return jax.ShapeDtypeStruct(shape, kind)


def deal_kernel(tokens_ref, upstream_ref, out_ref, *, quarters):
    part = tokens_ref.shape[1] // quarters
    for q in range(quarters):
        rows = tokens_ref[:, q * part : (q + 1) * part]
        grads = upstream_ref[:, q * part : (q + 1) * part]
        for j in range(out_ref.shape[0] // quarters):
            out_ref[j * quarters + q, :, :part] = rows
            out_ref[j * quarters + q, :, part:] = grads


def merge_kernel(blocks_ref, out_ref, rows_ref):
    n, pair, _ = blocks_ref.shape
    for j in range(n):
        rows_ref[j * pair : (j + 1) * pair, :] = blocks_ref[j].astype(F32)
    out_ref[...] = rows_ref[...].astype(BF16)


def pack_kernel(_, gate_ref, up_ref, down_ref, out_ref):
    units = gate_ref.shape[0]
    for j, ref in enumerate((gate_ref, up_ref, down_ref)):
        out_ref[j * units : (j + 1) * units, :] = ref[...]


def weights_kernel(_, gate_ref, up_ref, down_ref, got_ref, in_ref, out_ref):
    units = gate_ref.shape[0]
    in_ref[:units, :] = gate_ref[...]
    in_ref[units : 2 * units, :] = up_ref[...]
    in_ref[2 * units :, :] = got_ref[: 2 * units, :]
    out_ref[:units, :] = down_ref[...]
    out_ref[units:, :] = got_ref[2 * units :, :]


def stack_kernel(*refs):
    *block_refs, rows_ref, grads_ref = refs
    part = rows_ref.shape[1]
    k = 0
    for ref in block_refs:
        height, width = ref.shape
        at = slice(k * height, (k + 1) * height)
        if width == 2 * part:
            rows_ref[at, :] = ref[:, :part]
            grads_ref[at, :] = ref[:, part:]
            k += 1
        elif ref is block_refs[-2]:
            rows_ref[at, :] = ref[...]
        else:
            grads_ref[at, :] = ref[...]
            k += 1


def partial_kernel(rows_ref, grads_ref, in_ref, out_ref, own_ref, other_ref):
    units = out_ref.shape[0] // 2
    rows, grads = rows_ref[...], grads_ref[...]
    for j, ref in enumerate((own_ref, other_ref)):
        ref[: 2 * units, :] = by_rows(in_ref[2 * j * units : 2 * (j + 1) * units, :], rows)
        ref[2 * units :, :] = by_rows(out_ref[j * units : (j + 1) * units, :], grads)


def middle_kernel(sum_ref, got_ref, out_ref):
    units = sum_ref.shape[0] // 3
    total = sum_ref[...] + got_ref[...]
    gate_value, up_value = total[:units, :], total[units : 2 * units, :]
    hidden_grad = total[2 * units :, :]
    gate_sigmoid = jax.nn.sigmoid(gate_value)
    swish_gate = gate_value * gate_sigmoid
    gate_grad = hidden_grad * up_value * gate_sigmoid * (1.0 + gate_value * (1.0 - gate_sigmoid))
    out_ref[:units, :] = gate_grad.astype(BF16)
    out_ref[units : 2 * units, :] = (hidden_grad * swish_gate).astype(BF16)
    out_ref[2 * units :, :] = (swish_gate * up_value).astype(BF16)


def pair_kernel(own_ref, got_ref, in_ref, hidden_ref):
    double = in_ref.shape[0] // 2
    in_ref[:double, :] = own_ref[:double, :]
    in_ref[double:, :] = got_ref[:double, :]
    hidden_ref[: double // 2, :] = own_ref[double:, :]
    hidden_ref[double // 2 :, :] = got_ref[double:, :]


def turn_kernel(_, term_ref, came_ref, out_ref):
    out_ref[...] = (term_ref[...] + came_ref[...].astype(F32)).astype(BF16)


def close_kernel(_, a0_ref, b0_ref, a1_ref, a2_ref, b1_ref, b2_ref, out_ref, rows_ref):
    n, pair, _ = out_ref.shape
    width = a0_ref.shape[1]
    rows_ref[:, :width] = a0_ref[...] + a1_ref[...].astype(F32) + a2_ref[...].astype(F32)
    rows_ref[:, width:] = b0_ref[...] + b1_ref[...].astype(F32) + b2_ref[...].astype(F32)
    for j in range(n):
        out_ref[j] = rows_ref[j * pair : (j + 1) * pair, :].astype(BF16)


def total_kernel(blocks_ref, mixed_ref, input_ref, *, quarters):
    part = mixed_ref.shape[1] // quarters
    for q in range(quarters):
        total = blocks_ref[q].astype(F32)
        for j in range(1, blocks_ref.shape[0] // quarters):
            total = total + blocks_ref[j * quarters + q].astype(F32)
        total = total.astype(BF16)
        mixed_ref[:, q * part : (q + 1) * part] = total[:, :part]
        input_ref[:, q * part : (q + 1) * part] = total[:, part:]


def ring_reduced(terms, later, height, pair):
    count = lax.axis_size("z")
    half = count // 2

    def at(k):
        found, j = terms[k % count]
        place = ((height, found[0].shape[1]), lambda *_: (j, 0))
        return found, place

    def own_term(ring, k):
        found, j = terms[k % count]
        return found[ring][j * height : (j + 1) * height].astype(BF16)

    def turned(ring, k, came):
        if came is None:
            return own_term(ring, k)
        found, place = at(k)
        out = shape_of((height, found[ring].shape[1]))
        return called_at(turn_kernel, out, [place, None], found[ring], came)

    def sent(block, distance):
        return None if block is None else shifted(block, "z", distance)

    width = terms[half][0][0].shape[1]
    rings = [[own_term(0, half), None], [None, own_term(1, half)]]
    for k in range(half - 1, 0, -1):
        for j, (up, down) in enumerate(rings):
            rings[j] = [sent(up, 1), sent(down, -1)]
        if k in later:
            rings[0][0], rings[0][1] = later[k](*rings[0])
        for j, (up, down) in enumerate(rings):
            rings[j] = [turned(j, k, up), turned(j, -k, down)]
    came = [c for up, down in rings for c in (shifted(up, "z", 1), shifted(down, "z", -1))]
    found, place = at(0)
    return called_at(
        close_kernel,
        shape_of((height // pair, pair, 2 * width)),
        [place, place] + [None] * len(came),
        *found,
        *came,
        scratch=[pltpu.VMEM((height, 2 * width), F32)],
    )


def local(tokens, upstream, gate_weight, up_weight, down_weight):
    core = lax.axis_index("core")
    tok = lax.axis_index("tok")
    n_z = lax.axis_size("z")
    n_plane = lax.axis_size("y") * lax.axis_size("x")
    n_core = lax.axis_size("core")
    quarters = n_core * lax.axis_size("tok")
    pair, width = tokens.shape
    part = width // quarters
    units = gate_weight.shape[0]
    n = pair * quarters
    n_rows = n_plane * n
    own_at = (tok * n_core + core).astype(jnp.int32).reshape(1)
    other_at = (tok * n_core + 1 - core).astype(jnp.int32).reshape(1)

    dealt = called(
        deal_kernel,
        shape_of((n_plane * quarters, pair, 2 * part)),
        tokens,
        upstream,
        quarters=quarters,
    )
    dealt, *weights = lax.optimization_barrier((dealt, gate_weight, up_weight, down_weight))
    column = ((units, part), lambda i, at: (0, at[0]))
    sent = called_at(
        pack_kernel,
        shape_of((3 * units, part)),
        [column] * 3,
        *weights,
        index=other_at,
        params=LARGE,
    )
    in_weights, out_weights = called_at(
        weights_kernel,
        (shape_of((4 * units, part)), shape_of((2 * units, part))),
        [column] * 3 + [None],
        *weights,
        shifted(sent, "core", 1),
        index=own_at,
        params=LARGE,
    )
    dealt = exchanged(dealt, (*PLANE, *PAIRS))
    dealt, in_weights, out_weights = lax.optimization_barrier((dealt, in_weights, out_weights))
    block = called(
        merge_kernel,
        shape_of((n_rows, 2 * part)),
        dealt,
        scratch=[pltpu.VMEM((n_rows, 2 * part), F32)],
    )

    def stacked(*blocks):
        shape = shape_of((half * n_rows, part))
        return called(stack_kernel, (shape, shape), *blocks)

    def partial_sums(rows, grads):
        shape = shape_of((3 * units, rows.shape[0]), F32)
        return called(partial_kernel, (shape, shape), rows, grads, in_weights, out_weights)

    def factors(sums, got):
        own = called(middle_kernel, shape_of(sums.shape), sums, got)
        return called(
            pair_kernel,
            (
                shape_of((4 * units, sums.shape[1])),
                shape_of((2 * units, sums.shape[1])),
            ),
            own,
            shifted(own, "core", 1),
        )

    half = n_z // 2
    ring = {0: block}
    for k in range(1, half):
        ring[k], ring[-k] = shifted(ring[k - 1], "z", -1), shifted(ring[1 - k], "z", 1)
    near_rows, near_grads = stacked(*(ring[k] for k in range(-half // 2, half // 2)))
    own, other = partial_sums(near_rows, near_grads)
    near_sums = own + shifted(other, "core", 1)
    ahead, behind, near_sums = lax.optimization_barrier((ring[half - 1], ring[1 - half], near_sums))
    left, right = shifted(ahead[:, :part], "z", -1), shifted(behind[:, part:], "z", 1)
    near_got = shifted(near_sums, "tok", 1)
    left, right, near_got = lax.optimization_barrier((left, right, near_got))
    far_rows, far_grads = stacked(
        *(ring[k] for k in range(half // 2, half)),
        *(ring[k] for k in range(1 - half, -half // 2)),
        left,
        right,
    )
    own, other = partial_sums(far_rows, far_grads)
    far_sums = own + shifted(other, "core", 1)
    far_got = shifted(far_sums, "tok", 1)
    near_in, near_hidden = factors(near_sums, near_got)
    far_got, near_in, near_hidden = lax.optimization_barrier((far_got, near_in, near_hidden))
    far_in, far_hidden = factors(far_sums, far_got)

    terms = {}

    def set_terms(places, hidden, in_grads):
        found = (by_columns(hidden, out_weights), by_columns(in_grads, in_weights))
        for j, k in enumerate(places):
            terms[k % n_z] = found, j

    far_places = [*range(half // 2, half), *range(1 - half, -half // 2), half]
    set_terms(far_places, far_hidden, far_in)
    grads_out = []

    def near_terms(up, down):
        nonlocal near_in, near_hidden
        up, down, near_in, near_hidden = lax.optimization_barrier(
            (up, down, near_in, near_hidden)
        )
        set_terms(range(-half // 2, half // 2), near_hidden, near_in)
        return up, down

    def weight_product(near, far, near_right, far_right):
        total = jnp.dot(near, near_right, preferred_element_type=F32)
        total = total + jnp.dot(far, far_right, preferred_element_type=F32)
        return total.astype(BF16)

    def others_grads(up, down):
        up, down, a, b, c, d = lax.optimization_barrier(
            (up, down, near_in, far_in, near_hidden, far_hidden)
        )
        in_other = weight_product(a[2 * units :], b[2 * units :], near_rows, far_rows)
        out_other = weight_product(c[units:], d[units:], near_grads, far_grads)
        grads_out.extend([shifted(in_other, "core", 1), shifted(out_other, "core", 1)])
        return up, down

    later = {half - 1: near_terms, half - 2: others_grads}
    summed, a, b, c, d = lax.optimization_barrier(
        (
            ring_reduced(terms, later, n_rows, pair),
            near_in,
            far_in,
            near_hidden,
            far_hidden,
        )
    )
    in_weight_grad = weight_product(a[: 2 * units], b[: 2 * units], near_rows, far_rows)
    out_weight_grad = weight_product(c[:units], d[:units], near_grads, far_grads)
    mixed, input_grad = called(
        total_kernel,
        (shape_of((pair, width)), shape_of((pair, width))),
        exchanged(summed, (*PLANE, *PAIRS)),
        quarters=quarters,
    )
    got_in, got_out = grads_out

    def side_by_side(mine, others):
        left = jnp.where(core == 0, mine, others)
        right = jnp.where(core == 0, others, mine)
        return jnp.concatenate([left, right], axis=1)

    return (
        mixed,
        input_grad,
        side_by_side(in_weight_grad[:units], got_in[:units]),
        side_by_side(in_weight_grad[units:], got_in[units:]),
        side_by_side(out_weight_grad, got_out),
    )


def solution(mesh):
    finer = Mesh(mesh.devices.reshape(8, 4, 2, 2, mesh.shape["tok"]), AXES)
    return jax.shard_map(
        local,
        mesh=finer,
        in_specs=(P(AXES, None), P(AXES, None), P(BLK, None), P(BLK, None), P(BLK, None)),
        out_specs=(P(AXES, None), P(AXES, None), P(BLK, "tok"), P(BLK, "tok"), P(BLK, "tok")),
        check_vma=False,
    )
```

```python
import functools

import jax
import jax.numpy as jnp
from jax import lax
from jax.experimental import pallas as pl
from jax.experimental.pallas import tpu as pltpu
from jax.sharding import Mesh
from jax.sharding import PartitionSpec as P

AXES = ("z", "y", "x", "core", "tok")
BLK = ("z", "y", "x", "core")
PLANE = ("y", "x")
PAIRS = ("tok", "core")
F32 = jnp.float32
BF16 = jnp.bfloat16
VMEM = pl.BlockSpec(memory_space=pltpu.VMEM)
SMEM = pl.BlockSpec(memory_space=pltpu.SMEM)
PARAMS = pltpu.CompilerParams(vmem_limit_bytes=20 * 1024 * 1024)
LARGE = pltpu.CompilerParams(vmem_limit_bytes=58 * 1024 * 1024)


def shifted(block, axis, distance):
    count = lax.axis_size(axis)
    return lax.ppermute(block, axis, [(i, (i + distance) % count) for i in range(count)])


def exchanged(blocks, axes):
    return lax.all_to_all(blocks, axes, 0, 0, tiled=True)


def by_rows(left, right):
    return lax.dot_general(left, right, (((1,), (1,)), ((), ())), preferred_element_type=F32)


def by_columns(left, right):
    return lax.dot_general(left, right, (((0,), (0,)), ((), ())), preferred_element_type=F32)


def called(kernel, out_shape, *args, specs=None, scratch=(), **kwargs):
    specs = specs or [VMEM] * len(args)
    return pl.pallas_call(
        functools.partial(kernel, **kwargs),
        out_shape=out_shape,
        in_specs=specs,
        out_specs=jax.tree.map(lambda _: VMEM, out_shape),
        scratch_shapes=scratch,
        compiler_params=PARAMS,
    )(*args)


def called_at(kernel, out_shape, places, *args, index=None, scratch=(), params=PARAMS, **kwargs):
    def whole(shape):
        return pl.BlockSpec(shape, lambda *_: (0,) * len(shape))

    specs = [
        whole(arg.shape) if place is None else pl.BlockSpec(*place)
        for arg, place in zip(args, places, strict=True)
    ]
    grid = pltpu.PrefetchScalarGridSpec(
        num_scalar_prefetch=1,
        grid=(1,),
        in_specs=specs,
        out_specs=jax.tree.map(lambda o: whole(o.shape), out_shape),
        scratch_shapes=scratch,
    )
    return pl.pallas_call(
        functools.partial(kernel, **kwargs),
        out_shape=out_shape,
        grid_spec=grid,
        compiler_params=params,
    )(jnp.zeros((1,), jnp.int32) if index is None else index, *args)


def shape_of(shape, kind=BF16):
    return jax.ShapeDtypeStruct(shape, kind)


def copy_rows(dst, src, at, start, count):
    def some(i, carry):
        to = pl.ds(pl.multiple_of(at + i * 16, 16), 16)
        dst[to, :] = src[pl.ds(pl.multiple_of(start + i * 16, 16), 16), :]
        return carry

    lax.fori_loop(0, count // 16, some, 0)


def deal_kernel(tokens_ref, upstream_ref, out_ref, *, quarters):
    part = tokens_ref.shape[1] // quarters
    for q in range(quarters):
        rows = tokens_ref[:, q * part : (q + 1) * part]
        grads = upstream_ref[:, q * part : (q + 1) * part]
        for j in range(out_ref.shape[0] // quarters):
            out_ref[j * quarters + q, :, :part] = rows
            out_ref[j * quarters + q, :, part:] = grads


def merge_kernel(blocks_ref, left_ref, right_ref, rows_ref):
    n, pair, _ = blocks_ref.shape
    for j in range(n):
        rows_ref[j * pair : (j + 1) * pair, :] = blocks_ref[j].astype(F32)
    left_ref[...] = rows_ref[:, : left_ref.shape[1]].astype(BF16)
    right_ref[...] = rows_ref[:, left_ref.shape[1] :].astype(BF16)


def pack_kernel(_, gate_ref, up_ref, down_ref, out_ref):
    units = gate_ref.shape[0]
    for j, ref in enumerate((gate_ref, up_ref, down_ref)):
        copy_rows(out_ref, ref, j * units, 0, units)


def weights_kernel(_, gate_ref, up_ref, down_ref, got_ref, in_ref, out_ref):
    units = gate_ref.shape[0]
    copy_rows(in_ref, gate_ref, 0, 0, units)
    copy_rows(in_ref, up_ref, units, 0, units)
    copy_rows(in_ref, got_ref, 2 * units, 0, 2 * units)
    copy_rows(out_ref, down_ref, 0, 0, units)
    copy_rows(out_ref, got_ref, units, 2 * units, units)


def stack_kernel(*refs):
    *block_refs, out_ref = refs
    for k, ref in enumerate(block_refs):
        copy_rows(out_ref, ref, k * ref.shape[0], 0, ref.shape[0])


def partial_kernel(rows_ref, grads_ref, in_ref, out_ref, own_ref, other_ref):
    units = out_ref.shape[0] // 2
    rows, grads = rows_ref[...], grads_ref[...]
    for j, ref in enumerate((own_ref, other_ref)):
        ref[: 2 * units, :] = by_rows(in_ref[2 * j * units : 2 * (j + 1) * units, :], rows)
        ref[2 * units :, :] = by_rows(out_ref[j * units : (j + 1) * units, :], grads)


def middle_kernel(sum_ref, got_ref, out_ref):
    units = sum_ref.shape[0] // 3
    total = sum_ref[...] + got_ref[...]
    gate_value, up_value = total[:units, :], total[units : 2 * units, :]
    hidden_grad = total[2 * units :, :]
    gate_sigmoid = jax.nn.sigmoid(gate_value)
    swish_gate = gate_value * gate_sigmoid
    gate_grad = hidden_grad * up_value * gate_sigmoid * (1.0 + gate_value * (1.0 - gate_sigmoid))
    out_ref[:units, :] = gate_grad.astype(BF16)
    out_ref[units : 2 * units, :] = (hidden_grad * swish_gate).astype(BF16)
    out_ref[2 * units :, :] = (swish_gate * up_value).astype(BF16)


def pair_kernel(own_ref, got_ref, in_ref, hidden_ref):
    double = in_ref.shape[0] // 2
    in_ref[:double, :] = own_ref[:double, :]
    in_ref[double:, :] = got_ref[:double, :]
    hidden_ref[: double // 2, :] = own_ref[double:, :]
    hidden_ref[double // 2 :, :] = got_ref[double:, :]


def turn_kernel(_, term_ref, came_ref, out_ref):
    def some(i, carry):
        at = pl.ds(pl.multiple_of(i * 16, 16), 16)
        out_ref[at, :] = (term_ref[at, :] + came_ref[at, :].astype(F32)).astype(BF16)
        return carry

    lax.fori_loop(0, term_ref.shape[0] // 16, some, 0)


def close_kernel(_, a0_ref, b0_ref, a1_ref, a2_ref, b1_ref, b2_ref, out_ref, rows_ref):
    n, pair, _ = out_ref.shape
    width = a0_ref.shape[1]
    rows_ref[:, :width] = a0_ref[...] + a1_ref[...].astype(F32) + a2_ref[...].astype(F32)
    rows_ref[:, width:] = b0_ref[...] + b1_ref[...].astype(F32) + b2_ref[...].astype(F32)
    for j in range(n):
        out_ref[j] = rows_ref[j * pair : (j + 1) * pair, :].astype(BF16)


def total_kernel(blocks_ref, mixed_ref, input_ref, *, quarters):
    part = mixed_ref.shape[1] // quarters
    for q in range(quarters):
        total = blocks_ref[q].astype(F32)
        for j in range(1, blocks_ref.shape[0] // quarters):
            total = total + blocks_ref[j * quarters + q].astype(F32)
        total = total.astype(BF16)
        mixed_ref[:, q * part : (q + 1) * part] = total[:, :part]
        input_ref[:, q * part : (q + 1) * part] = total[:, part:]


def ring_reduced(terms, later, height, pair):
    count = lax.axis_size("z")
    half = count // 2

    def at(k):
        found, j = terms[k % count]
        place = ((height, found[0].shape[1]), lambda *_: (j, 0))
        return found, place

    def own_term(ring, k):
        found, j = terms[k % count]
        return found[ring][j * height : (j + 1) * height].astype(BF16)

    def turned(ring, k, came):
        if came is None:
            return own_term(ring, k)
        found, place = at(k)
        out = shape_of((height, found[ring].shape[1]))
        return called_at(turn_kernel, out, [place, None], found[ring], came)

    def sent(block, distance):
        return None if block is None else shifted(block, "z", distance)

    width = terms[half][0][0].shape[1]
    rings = [[own_term(0, half), None], [None, own_term(1, half)]]
    for k in range(half - 1, 0, -1):
        for j, (up, down) in enumerate(rings):
            rings[j] = [sent(up, 1), sent(down, -1)]
        if k in later:
            rings[0][0], rings[0][1] = later[k](*rings[0])
        for j, (up, down) in enumerate(rings):
            rings[j] = [turned(j, k, up), turned(j, -k, down)]
    came = [c for up, down in rings for c in (shifted(up, "z", 1), shifted(down, "z", -1))]
    found, place = at(0)
    return called_at(
        close_kernel,
        shape_of((height // pair, pair, 2 * width)),
        [place, place] + [None] * len(came),
        *found,
        *came,
        scratch=[pltpu.VMEM((height, 2 * width), F32)],
    )


def local(tokens, upstream, gate_weight, up_weight, down_weight):
    core = lax.axis_index("core")
    tok = lax.axis_index("tok")
    n_z = lax.axis_size("z")
    n_plane = lax.axis_size("y") * lax.axis_size("x")
    n_core = lax.axis_size("core")
    quarters = n_core * lax.axis_size("tok")
    pair, width = tokens.shape
    part = width // quarters
    units = gate_weight.shape[0]
    n = pair * quarters
    n_rows = n_plane * n
    own_at = (tok * n_core + core).astype(jnp.int32).reshape(1)
    other_at = (tok * n_core + 1 - core).astype(jnp.int32).reshape(1)

    dealt = called(
        deal_kernel,
        shape_of((n_plane * quarters, pair, 2 * part)),
        tokens,
        upstream,
        quarters=quarters,
    )
    dealt, *weights = lax.optimization_barrier((dealt, gate_weight, up_weight, down_weight))
    column = ((units, part), lambda i, at: (0, at[0]))
    sent = called_at(
        pack_kernel,
        shape_of((3 * units, part)),
        [column] * 3,
        *weights,
        index=other_at,
        params=LARGE,
    )
    in_weights, out_weights = called_at(
        weights_kernel,
        (shape_of((4 * units, part)), shape_of((2 * units, part))),
        [column] * 3 + [None],
        *weights,
        shifted(sent, "core", 1),
        index=own_at,
        params=LARGE,
    )
    dealt = exchanged(dealt, (*PLANE, *PAIRS))
    dealt, in_weights, out_weights = lax.optimization_barrier((dealt, in_weights, out_weights))
    blocks = called(
        merge_kernel,
        (shape_of((n_rows, part)), shape_of((n_rows, part))),
        dealt,
        scratch=[pltpu.VMEM((n_rows, 2 * part), F32)],
    )

    def stacked(*blocks):
        return called(stack_kernel, shape_of((half * n_rows, part)), *blocks)

    def partial_sums(rows, grads):
        shape = shape_of((3 * units, rows.shape[0]), F32)
        return called(partial_kernel, (shape, shape), rows, grads, in_weights, out_weights)

    def factors(sums, got):
        own = called(middle_kernel, shape_of(sums.shape), sums, got)
        return called(
            pair_kernel,
            (
                shape_of((4 * units, sums.shape[1])),
                shape_of((2 * units, sums.shape[1])),
            ),
            own,
            shifted(own, "core", 1),
        )

    half = n_z // 2
    rings = [{0: block} for block in blocks]
    for k in range(1, half):
        for ring in rings:
            ring[k], ring[-k] = shifted(ring[k - 1], "z", -1), shifted(ring[1 - k], "z", 1)
    near_rows, near_grads = (
        stacked(*(ring[k] for k in range(-half // 2, half // 2))) for ring in rings
    )
    own, other = partial_sums(near_rows, near_grads)
    near_sums = own + shifted(other, "core", 1)
    ahead, behind = rings[0][half - 1], rings[1][1 - half]
    behind, near_sums = lax.optimization_barrier((behind, near_sums))
    near_got = shifted(near_sums, "tok", 1)
    *ends, near_got = lax.optimization_barrier(
        (shifted(ahead, "z", -1), shifted(behind, "z", 1), near_got)
    )
    far_rows, far_grads = (
        stacked(
            *(ring[k] for k in range(half // 2, half)),
            *(ring[k] for k in range(1 - half, -half // 2)),
            end,
        )
        for ring, end in zip(rings, ends, strict=True)
    )
    own, other = partial_sums(far_rows, far_grads)
    far_sums = own + shifted(other, "core", 1)
    far_got = shifted(far_sums, "tok", 1)
    near_in, near_hidden = factors(near_sums, near_got)
    far_got, near_in, near_hidden = lax.optimization_barrier((far_got, near_in, near_hidden))
    far_in, far_hidden = factors(far_sums, far_got)

    terms = {}

    def set_terms(places, hidden, in_grads):
        found = (by_columns(hidden, out_weights), by_columns(in_grads, in_weights))
        for j, k in enumerate(places):
            terms[k % n_z] = found, j

    far_places = [*range(half // 2, half), *range(1 - half, -half // 2), half]
    set_terms(far_places, far_hidden, far_in)
    grads_out = []

    def near_terms(up, down):
        nonlocal near_in, near_hidden
        up, down, near_in, near_hidden = lax.optimization_barrier(
            (up, down, near_in, near_hidden)
        )
        set_terms(range(-half // 2, half // 2), near_hidden, near_in)
        return up, down

    def weight_product(near, far, near_right, far_right):
        total = jnp.dot(near, near_right, preferred_element_type=F32)
        total = total + jnp.dot(far, far_right, preferred_element_type=F32)
        return total.astype(BF16)

    def others_grads(up, down):
        up, down, a, b, c, d = lax.optimization_barrier(
            (up, down, near_in, far_in, near_hidden, far_hidden)
        )
        in_other = weight_product(a[2 * units :], b[2 * units :], near_rows, far_rows)
        out_other = weight_product(c[units:], d[units:], near_grads, far_grads)
        grads_out.extend([shifted(in_other, "core", 1), shifted(out_other, "core", 1)])
        return up, down

    later = {half - 1: near_terms, half - 2: others_grads}
    summed, a, b, c, d = lax.optimization_barrier(
        (
            ring_reduced(terms, later, n_rows, pair),
            near_in,
            far_in,
            near_hidden,
            far_hidden,
        )
    )
    in_weight_grad = weight_product(a[: 2 * units], b[: 2 * units], near_rows, far_rows)
    out_weight_grad = weight_product(c[:units], d[:units], near_grads, far_grads)
    mixed, input_grad = called(
        total_kernel,
        (shape_of((pair, width)), shape_of((pair, width))),
        exchanged(summed, (*PLANE, *PAIRS)),
        quarters=quarters,
    )
    got_in, got_out = grads_out

    def side_by_side(mine, others):
        left = jnp.where(core == 0, mine, others)
        right = jnp.where(core == 0, others, mine)
        return jnp.concatenate([left, right], axis=1)

    return (
        mixed,
        input_grad,
        side_by_side(in_weight_grad[:units], got_in[:units]),
        side_by_side(in_weight_grad[units:], got_in[units:]),
        side_by_side(out_weight_grad, got_out),
    )


def solution(mesh):
    finer = Mesh(mesh.devices.reshape(8, 4, 2, 2, mesh.shape["tok"]), AXES)
    return jax.shard_map(
        local,
        mesh=finer,
        in_specs=(P(AXES, None), P(AXES, None), P(BLK, None), P(BLK, None), P(BLK, None)),
        out_specs=(P(AXES, None), P(AXES, None), P(BLK, "tok"), P(BLK, "tok"), P(BLK, "tok")),
        check_vma=False,
    )
```

```python
import functools

import jax
import jax.numpy as jnp
from jax import lax
from jax.experimental import pallas as pl
from jax.experimental.pallas import tpu as pltpu
from jax.sharding import Mesh
from jax.sharding import PartitionSpec as P

AXES = ("z", "y", "x", "core", "tok")
BLK = ("z", "y", "x", "core")
PLANE = ("y", "x")
PAIRS = ("tok", "core")
F32 = jnp.float32
BF16 = jnp.bfloat16
VMEM = pl.BlockSpec(memory_space=pltpu.VMEM)
SMEM = pl.BlockSpec(memory_space=pltpu.SMEM)
PARAMS = pltpu.CompilerParams(vmem_limit_bytes=20 * 1024 * 1024)
LARGE = pltpu.CompilerParams(vmem_limit_bytes=58 * 1024 * 1024)


def shifted(block, axis, distance):
    count = lax.axis_size(axis)
    return lax.ppermute(block, axis, [(i, (i + distance) % count) for i in range(count)])


def exchanged(blocks, axes):
    return lax.all_to_all(blocks, axes, 0, 0, tiled=True)


def by_rows(left, right):
    return lax.dot_general(left, right, (((1,), (1,)), ((), ())), preferred_element_type=F32)


def by_columns(left, right):
    return lax.dot_general(left, right, (((0,), (0,)), ((), ())), preferred_element_type=F32)


def called(kernel, out_shape, *args, specs=None, scratch=(), **kwargs):
    specs = specs or [VMEM] * len(args)
    return pl.pallas_call(
        functools.partial(kernel, **kwargs),
        out_shape=out_shape,
        in_specs=specs,
        out_specs=jax.tree.map(lambda _: VMEM, out_shape),
        scratch_shapes=scratch,
        compiler_params=PARAMS,
    )(*args)


def called_at(kernel, out_shape, places, *args, index=None, scratch=(), params=PARAMS, **kwargs):
    def whole(shape):
        return pl.BlockSpec(shape, lambda *_: (0,) * len(shape))

    specs = [
        whole(arg.shape) if place is None else pl.BlockSpec(*place)
        for arg, place in zip(args, places, strict=True)
    ]
    grid = pltpu.PrefetchScalarGridSpec(
        num_scalar_prefetch=1,
        grid=(1,),
        in_specs=specs,
        out_specs=jax.tree.map(lambda o: whole(o.shape), out_shape),
        scratch_shapes=scratch,
    )
    return pl.pallas_call(
        functools.partial(kernel, **kwargs),
        out_shape=out_shape,
        grid_spec=grid,
        compiler_params=params,
    )(jnp.zeros((1,), jnp.int32) if index is None else index, *args)


def shape_of(shape, kind=BF16):
    return jax.ShapeDtypeStruct(shape, kind)


def copy_rows(dst, src, at, start, count):
    def some(i, carry):
        to = pl.ds(pl.multiple_of(at + i * 16, 16), 16)
        dst[to, :] = src[pl.ds(pl.multiple_of(start + i * 16, 16), 16), :]
        return carry

    lax.fori_loop(0, count // 16, some, 0)


def deal_kernel(tokens_ref, upstream_ref, out_ref, *, quarters):
    part = tokens_ref.shape[1] // quarters
    for q in range(quarters):
        rows = tokens_ref[:, q * part : (q + 1) * part]
        grads = upstream_ref[:, q * part : (q + 1) * part]
        for j in range(out_ref.shape[0] // quarters):
            out_ref[j * quarters + q, :, :part] = rows
            out_ref[j * quarters + q, :, part:] = grads


def merge_kernel(blocks_ref, left_ref, right_ref, rows_ref):
    n, pair, _ = blocks_ref.shape
    for j in range(n):
        rows_ref[j * pair : (j + 1) * pair, :] = blocks_ref[j].astype(F32)
    left_ref[...] = rows_ref[:, : left_ref.shape[1]].astype(BF16)
    right_ref[...] = rows_ref[:, left_ref.shape[1] :].astype(BF16)


def pack_kernel(_, gate_ref, up_ref, down_ref, out_ref):
    units = gate_ref.shape[0]
    for j, ref in enumerate((gate_ref, up_ref, down_ref)):
        copy_rows(out_ref, ref, j * units, 0, units)


def weights_kernel(_, gate_ref, up_ref, down_ref, got_ref, in_ref, out_ref):
    units = gate_ref.shape[0]
    copy_rows(in_ref, gate_ref, 0, 0, units)
    copy_rows(in_ref, up_ref, units, 0, units)
    copy_rows(in_ref, got_ref, 2 * units, 0, 2 * units)
    copy_rows(out_ref, down_ref, 0, 0, units)
    copy_rows(out_ref, got_ref, units, 2 * units, units)


def stack_kernel(*refs):
    *block_refs, out_ref = refs
    for k, ref in enumerate(block_refs):
        copy_rows(out_ref, ref, k * ref.shape[0], 0, ref.shape[0])


def partial_kernel(rows_ref, grads_ref, in_ref, out_ref, own_ref, other_ref):
    units = out_ref.shape[0] // 2
    rows, grads = rows_ref[...], grads_ref[...]
    for j, ref in enumerate((own_ref, other_ref)):
        ref[: 2 * units, :] = by_rows(in_ref[2 * j * units : 2 * (j + 1) * units, :], rows)
        ref[2 * units :, :] = by_rows(out_ref[j * units : (j + 1) * units, :], grads)


def middle_kernel(sum_ref, got_ref, out_ref):
    units = sum_ref.shape[0] // 3
    total = sum_ref[...] + got_ref[...]
    gate_value, up_value = total[:units, :], total[units : 2 * units, :]
    hidden_grad = total[2 * units :, :]
    gate_sigmoid = jax.nn.sigmoid(gate_value)
    swish_gate = gate_value * gate_sigmoid
    gate_grad = hidden_grad * up_value * gate_sigmoid * (1.0 + gate_value * (1.0 - gate_sigmoid))
    out_ref[:units, :] = gate_grad.astype(BF16)
    out_ref[units : 2 * units, :] = (hidden_grad * swish_gate).astype(BF16)
    out_ref[2 * units :, :] = (swish_gate * up_value).astype(BF16)


def pair_kernel(own_ref, got_ref, in_ref, hidden_ref):
    double = in_ref.shape[0] // 2
    in_ref[:double, :] = own_ref[:double, :]
    in_ref[double:, :] = got_ref[:double, :]
    hidden_ref[: double // 2, :] = own_ref[double:, :]
    hidden_ref[double // 2 :, :] = got_ref[double:, :]


def turn_kernel(_, term_ref, came_ref, out_ref):
    def some(i, carry):
        at = pl.ds(pl.multiple_of(i * 16, 16), 16)
        out_ref[at, :] = (term_ref[at, :] + came_ref[at, :].astype(F32)).astype(BF16)
        return carry

    lax.fori_loop(0, term_ref.shape[0] // 16, some, 0)


def close_kernel(_, a0_ref, b0_ref, a1_ref, a2_ref, b1_ref, b2_ref, out_ref, rows_ref):
    n, pair, _ = out_ref.shape
    width = a0_ref.shape[1]
    rows_ref[:, :width] = a0_ref[...] + a1_ref[...].astype(F32) + a2_ref[...].astype(F32)
    rows_ref[:, width:] = b0_ref[...] + b1_ref[...].astype(F32) + b2_ref[...].astype(F32)
    for j in range(n):
        out_ref[j] = rows_ref[j * pair : (j + 1) * pair, :].astype(BF16)


def total_kernel(blocks_ref, mixed_ref, input_ref, *, quarters):
    part = mixed_ref.shape[1] // quarters
    for q in range(quarters):
        total = blocks_ref[q].astype(F32)
        for j in range(1, blocks_ref.shape[0] // quarters):
            total = total + blocks_ref[j * quarters + q].astype(F32)
        total = total.astype(BF16)
        mixed_ref[:, q * part : (q + 1) * part] = total[:, :part]
        input_ref[:, q * part : (q + 1) * part] = total[:, part:]


def ring_reduced(terms, later, height, pair):
    count = lax.axis_size("z")
    half = count // 2

    def at(k):
        found, j = terms[k % count]
        place = ((height, found[0].shape[1]), lambda *_: (j, 0))
        return found, place

    def own_term(ring, k):
        found, j = terms[k % count]
        return found[ring][j * height : (j + 1) * height].astype(BF16)

    def turned(ring, k, came):
        if came is None:
            return own_term(ring, k)
        found, place = at(k)
        out = shape_of((height, found[ring].shape[1]))
        return called_at(turn_kernel, out, [place, None], found[ring], came)

    def sent(block, distance):
        return None if block is None else shifted(block, "z", distance)

    width = terms[half][0][0].shape[1]
    rings = [[own_term(0, half), None], [None, own_term(1, half)]]
    for k in range(half - 1, 0, -1):
        for j, (up, down) in enumerate(rings):
            rings[j] = [sent(up, 1), sent(down, -1)]
        if k in later:
            rings[0][0], rings[0][1] = later[k](*rings[0])
        for j, (up, down) in enumerate(rings):
            rings[j] = [turned(j, k, up), turned(j, -k, down)]
    came = [c for up, down in rings for c in (shifted(up, "z", 1), shifted(down, "z", -1))]
    found, place = at(0)
    return called_at(
        close_kernel,
        shape_of((height // pair, pair, 2 * width)),
        [place, place] + [None] * len(came),
        *found,
        *came,
        scratch=[pltpu.VMEM((height, 2 * width), F32)],
    )


def local(tokens, upstream, gate_weight, up_weight, down_weight):
    core = lax.axis_index("core")
    tok = lax.axis_index("tok")
    n_z = lax.axis_size("z")
    n_plane = lax.axis_size("y") * lax.axis_size("x")
    n_core = lax.axis_size("core")
    quarters = n_core * lax.axis_size("tok")
    pair, width = tokens.shape
    part = width // quarters
    units = gate_weight.shape[0]
    n = pair * quarters
    n_rows = n_plane * n
    own_at = (tok * n_core + core).astype(jnp.int32).reshape(1)
    other_at = (tok * n_core + 1 - core).astype(jnp.int32).reshape(1)

    dealt = called(
        deal_kernel,
        shape_of((n_plane * quarters, pair, 2 * part)),
        tokens,
        upstream,
        quarters=quarters,
    )
    dealt, *weights = lax.optimization_barrier((dealt, gate_weight, up_weight, down_weight))
    column = ((units, part), lambda i, at: (0, at[0]))
    sent = called_at(
        pack_kernel,
        shape_of((3 * units, part)),
        [column] * 3,
        *weights,
        index=other_at,
        params=LARGE,
    )
    in_weights, out_weights = called_at(
        weights_kernel,
        (shape_of((4 * units, part)), shape_of((2 * units, part))),
        [column] * 3 + [None],
        *weights,
        shifted(sent, "core", 1),
        index=own_at,
        params=LARGE,
    )
    dealt = exchanged(dealt, (*PLANE, *PAIRS))
    dealt, in_weights, out_weights = lax.optimization_barrier((dealt, in_weights, out_weights))
    blocks = called(
        merge_kernel,
        (shape_of((n_rows, part)), shape_of((n_rows, part))),
        dealt,
        scratch=[pltpu.VMEM((n_rows, 2 * part), F32)],
    )

    def stacked(*blocks):
        return called(stack_kernel, shape_of((half * n_rows, part)), *blocks)

    def partial_sums(rows, grads):
        shape = shape_of((3 * units, rows.shape[0]), F32)
        return called(partial_kernel, (shape, shape), rows, grads, in_weights, out_weights)

    def factors(sums, got):
        own = called(middle_kernel, shape_of(sums.shape), sums, got)
        return called(
            pair_kernel,
            (
                shape_of((4 * units, sums.shape[1])),
                shape_of((2 * units, sums.shape[1])),
            ),
            own,
            shifted(own, "core", 1),
        )

    half = n_z // 2
    rings = [{0: block} for block in blocks]
    for k in range(1, half):
        for ring in rings:
            ring[k], ring[-k] = shifted(ring[k - 1], "z", -1), shifted(ring[1 - k], "z", 1)
    near_rows, near_grads = (
        stacked(*(ring[k] for k in range(-half // 2, half // 2))) for ring in rings
    )
    own, other = partial_sums(near_rows, near_grads)
    near_sums = own + shifted(other, "core", 1)
    ahead, behind = rings[0][half - 1], rings[1][1 - half]
    ahead, near_sums = lax.optimization_barrier((ahead, near_sums))
    near_got = shifted(near_sums, "tok", 1)
    *ends, near_got = lax.optimization_barrier(
        (shifted(ahead, "z", -1), shifted(behind, "z", 1), near_got)
    )
    far_rows, far_grads = (
        stacked(
            *(ring[k] for k in range(half // 2, half)),
            *(ring[k] for k in range(1 - half, -half // 2)),
            end,
        )
        for ring, end in zip(rings, ends, strict=True)
    )
    own, other = partial_sums(far_rows, far_grads)
    far_sums = own + shifted(other, "core", 1)
    far_got = shifted(far_sums, "tok", 1)
    near_in, near_hidden = factors(near_sums, near_got)
    far_got, near_in, near_hidden = lax.optimization_barrier((far_got, near_in, near_hidden))
    far_in, far_hidden = factors(far_sums, far_got)

    terms = {}

    def set_terms(places, hidden, in_grads):
        found = (by_columns(hidden, out_weights), by_columns(in_grads, in_weights))
        for j, k in enumerate(places):
            terms[k % n_z] = found, j

    far_places = [*range(half // 2, half), *range(1 - half, -half // 2), half]
    set_terms(far_places, far_hidden, far_in)
    grads_out = []

    def near_terms(up, down):
        nonlocal near_in, near_hidden
        up, down, near_in, near_hidden = lax.optimization_barrier(
            (up, down, near_in, near_hidden)
        )
        set_terms(range(-half // 2, half // 2), near_hidden, near_in)
        return up, down

    def weight_product(near, far, near_right, far_right):
        total = jnp.dot(near, near_right, preferred_element_type=F32)
        total = total + jnp.dot(far, far_right, preferred_element_type=F32)
        return total.astype(BF16)

    def others_grads(up, down):
        up, down, a, b, c, d = lax.optimization_barrier(
            (up, down, near_in, far_in, near_hidden, far_hidden)
        )
        in_other = weight_product(a[2 * units :], b[2 * units :], near_rows, far_rows)
        out_other = weight_product(c[units:], d[units:], near_grads, far_grads)
        grads_out.extend([shifted(in_other, "core", 1), shifted(out_other, "core", 1)])
        return up, down

    later = {half - 1: near_terms, half - 2: others_grads}
    summed, a, b, c, d = lax.optimization_barrier(
        (
            ring_reduced(terms, later, n_rows, pair),
            near_in,
            far_in,
            near_hidden,
            far_hidden,
        )
    )
    in_weight_grad = weight_product(a[: 2 * units], b[: 2 * units], near_rows, far_rows)
    out_weight_grad = weight_product(c[:units], d[:units], near_grads, far_grads)
    mixed, input_grad = called(
        total_kernel,
        (shape_of((pair, width)), shape_of((pair, width))),
        exchanged(summed, (*PLANE, *PAIRS)),
        quarters=quarters,
    )
    got_in, got_out = grads_out

    def side_by_side(mine, others):
        left = jnp.where(core == 0, mine, others)
        right = jnp.where(core == 0, others, mine)
        return jnp.concatenate([left, right], axis=1)

    return (
        mixed,
        input_grad,
        side_by_side(in_weight_grad[:units], got_in[:units]),
        side_by_side(in_weight_grad[units:], got_in[units:]),
        side_by_side(out_weight_grad, got_out),
    )


def solution(mesh):
    finer = Mesh(mesh.devices.reshape(8, 4, 2, 2, mesh.shape["tok"]), AXES)
    return jax.shard_map(
        local,
        mesh=finer,
        in_specs=(P(AXES, None), P(AXES, None), P(BLK, None), P(BLK, None), P(BLK, None)),
        out_specs=(P(AXES, None), P(AXES, None), P(BLK, "tok"), P(BLK, "tok"), P(BLK, "tok")),
        check_vma=False,
    )
```
